32 devices in a mesh: tm: 16 (over z, y, x), mp: 2 (over core).
Axes of the slice: x: 2, y: 2, z: 4, core: 2. Of those that a mesh axis runs over, the one named last changes fastest.
Arguments:
- frames: bfloat16 [5120, 1024], P('tm'), may hold values from -6 to 6
- valid: int32 [5120], P('tm'), may hold values from 0 to 1, as said below
- norm_gain: float32 [1024], replicated, may hold values from 0.1 to 1.9
- norm_bias: float32 [1024], replicated, may hold values from -3 to 3
- w_qkv: bfloat16 [3, 1024, 1024], P(None, None, 'mp'), may hold values from -8 to 8
- w_out: bfloat16 [1024, 1024], P(None, 'mp'), may hold values from -0.1875 to 0.1875
- conv_weight: float32 [9, 1024], P(None, 'mp'), may hold values from -2 to 2
- conv_scale: float32 [1024], P('mp'), may hold values from 0.5 to 2
- conv_shift: float32 [1024], P('mp'), may hold values from -3 to 3
Outputs:
- encoded: bfloat16 [5120, 1024], P('tm', 'mp')
The draws below stay inside these ranges and needn't reach their ends.
Inputs may be any that keep to these rules, and one draw needn't show every extreme that they name: valid is 1 on a prefix of the frames and 0 on a final run of 1 to 128 frames.
All inputs are finite; a program needn't handle non-finite values.
Results may differ from the reference program's by a relative error of at most 0.0059.
Values may be sent and summed in bfloat16 or wider, within the bound.
No kernel may reach another device: no remote copies, remote signals or barrier semaphores. Data moves between devices by JAX's collectives and lax.ppermute only.
A program may use at most 64 MiB of HBM per device.

```python
import math
import jax
import jax.numpy as jnp
from jax import lax

D = 1024
HEADS = 8
HEAD_DIM = 128
CTX = 128
KERNEL = 9
FRAMES_DEV = 320
FRAMES = 5120
N_TM = 16


def draw_w_qkv(key, part):
    base = jax.random.normal(key, (3, D, D), jnp.float32) / math.sqrt(D)
    return jnp.clip(base, -8.0, 8.0).astype(jnp.bfloat16)


def draw_valid(key, part):
    tail = jax.random.randint(key, (), 1, CTX + 1)
    position = jnp.arange(FRAMES, dtype=jnp.int32)
    return (position < FRAMES - tail).astype(jnp.int32)


def block_scale(rng, extent, split, smallest, largest):
    loudness, own = 1.0, jax.random.fold_in(rng, 6)
    for axis_at, parts in split:
        draws = jnp.exp(jax.random.uniform(jax.random.fold_in(own, axis_at), (parts,), jnp.float32, smallest / len(split), largest / len(split)))
        loudness = loudness * jnp.repeat(draws, extent[axis_at] // parts).reshape([-1 if axis == axis_at else 1 for axis in range(len(extent))])
    return loudness


def centred(key, shape, scale, limit, pieces=(), held_as=jnp.bfloat16):
    loudness = block_scale(key, shape, pieces, -0.22, 0.18) if pieces else 1.0
    values = jax.random.normal(key, shape, jnp.float32) * scale * loudness
    return jnp.minimum(jnp.maximum(values, -limit), limit).astype(held_as)


def setup_inputs(seed: int = 0) -> dict:
    key_of = jax.random.split(jax.random.key(seed), 10)
    return {
        "frames": centred(key_of[0], (FRAMES, D), 1.0, 6.0, ((0, 16),)),
        "valid": draw_valid(jax.random.fold_in(key_of[9], 71), 0),
        "norm_gain": jnp.clip(1.0 + 0.18 * jax.random.normal(key_of[2], (D,), jnp.float32), 0.1, 1.9),
        "norm_bias": centred(key_of[3], (D,), 0.5, 3.0, (), jnp.float32),
        "w_qkv": draw_w_qkv(jax.random.fold_in(key_of[9], 71), 0),
        "w_out": centred(key_of[5], (D, D), D ** -0.5, 0.1875, ((1, 2),)),
        "conv_weight": centred(key_of[6], (KERNEL, D), KERNEL ** -0.5, 2.0, ((1, 2),), jnp.float32),
        "conv_scale": jnp.clip(jnp.exp(math.log(2.0) - 1.3862944 * jax.random.uniform(key_of[7], (D,), jnp.float32) ** block_scale(key_of[7], (D,), ((0, 2),), -0.2, 0.2)), 0.5, 2.0),
        "conv_shift": centred(key_of[8], (D,), 0.5, 3.0, ((0, 2),), jnp.float32),
    }


def layer_normed(frames, norm_gain, norm_bias):
    values = frames.astype(jnp.float32)
    center = values - lax.optimization_barrier(jnp.mean(values, axis=-1, keepdims=True))
    spread = lax.optimization_barrier(jnp.mean(center * center, axis=-1, keepdims=True))
    return (center * lax.rsqrt(spread + 1e-05) * norm_gain + norm_bias).astype(jnp.bfloat16)

def project(normed, matrix):
    return jnp.dot(normed, matrix, preferred_element_type=jnp.float32).astype(jnp.bfloat16)

def reference(frames, valid, norm_gain, norm_bias, w_qkv, w_out, conv_weight, conv_scale, conv_shift):
    normed = layer_normed(frames, norm_gain, norm_bias)
    queries = project(normed, w_qkv[0])
    keys = project(normed, w_qkv[1])
    values = project(normed, w_qkv[2])
    pad_keys = jnp.pad(keys, ((CTX, CTX), (0, 0)))
    pad_values = jnp.pad(values, ((CTX, CTX), (0, 0)))
    pad_valid = jnp.pad(valid.astype(jnp.float32), (CTX, CTX))
    scale = 1.0 / math.sqrt(HEAD_DIM)
    offset = jnp.arange(FRAMES_DEV + 2 * CTX, dtype=jnp.int32)[None, :] - jnp.arange(FRAMES_DEV, dtype=jnp.int32)[:, None]
    inside = (offset >= 0) & (offset <= 2 * CTX)

    def block(index):
        start = (index * FRAMES_DEV).astype(jnp.int32)
        query_block = lax.dynamic_slice_in_dim(queries, start, FRAMES_DEV, 0).astype(jnp.float32).reshape(FRAMES_DEV, HEADS, HEAD_DIM)
        key_block = lax.dynamic_slice_in_dim(pad_keys, start, FRAMES_DEV + 2 * CTX, 0).astype(jnp.float32).reshape(FRAMES_DEV + 2 * CTX, HEADS, HEAD_DIM)
        value_block = lax.dynamic_slice_in_dim(pad_values, start, FRAMES_DEV + 2 * CTX, 0).astype(jnp.float32).reshape(FRAMES_DEV + 2 * CTX, HEADS, HEAD_DIM)
        mark = lax.dynamic_slice_in_dim(pad_valid, start, FRAMES_DEV + 2 * CTX, 0)
        scores = jnp.einsum('thd,shd->hts', query_block, key_block) * scale
        allowed = inside & (mark[None, :] > 0.5)
        scores = jnp.where(allowed[None], scores, jnp.float32(-1e+30))
        top = lax.optimization_barrier(jnp.max(scores, axis=-1, keepdims=True))
        raised = jnp.exp(scores - top)
        weights = (raised / lax.optimization_barrier(jnp.sum(raised, axis=-1, keepdims=True))).astype(jnp.bfloat16)
        attended = jnp.einsum('hts,shd->thd', weights.astype(jnp.float32), value_block)
        return attended.astype(jnp.bfloat16).reshape(FRAMES_DEV, D)
    attended = lax.map(block, jnp.arange(N_TM, dtype=jnp.int32)).reshape(FRAMES, D)
    mixed = (frames.astype(jnp.float32) + jnp.dot(attended, w_out, preferred_element_type=jnp.float32)).astype(jnp.bfloat16)
    masked = mixed.astype(jnp.float32) * valid[:, None].astype(jnp.float32)
    half = KERNEL // 2
    padded = jnp.pad(masked, ((half, half), (0, 0)))
    conv = jnp.zeros((FRAMES, D), jnp.float32)
    for tap in range(KERNEL):
        conv = conv + padded[tap:tap + FRAMES] * conv_weight[tap]
    return (mixed.astype(jnp.float32) + jax.nn.silu(conv_scale * conv + conv_shift)).astype(jnp.bfloat16)
```

```python
import math

import jax
import jax.numpy as jnp
from jax import lax
from jax.experimental import pallas as pl
from jax.experimental.pallas import tpu as pltpu
from jax.sharding import PartitionSpec as P

HEAD_DIM = 128
CTX = 128
KERNEL = 9
EXT = 8
HALO = CTX + EXT
NEG = -1e30
SCALE = math.log2(math.e) / math.sqrt(HEAD_DIM)
VMEM = pl.BlockSpec(memory_space=pltpu.VMEM)


def layer_normed(values, gain, bias):
    center = values - jnp.mean(values, axis=-1, keepdims=True)
    spread = jnp.mean(center * center, axis=-1, keepdims=True)
    return center * lax.rsqrt(spread + 1e-05) * gain + bias


def dot(a, b):
    return jnp.dot(a, b, preferred_element_type=jnp.float32)


def dot_t(a, b):
    return lax.dot_general(a, b, (((1,), (1,)), ((), ())), preferred_element_type=jnp.float32)


def positions(shape, dim, start):
    return lax.broadcasted_iota(jnp.int32, shape, dim) + start


def own_kernel(
    frames, valid, gain, bias, w, q_out, k_out, v_out, top_out, total_out, acc_out, normed
):
    rows = frames.shape[0]
    p = lax.axis_index("mp")
    keys, queries = k_out.shape[0], q_out.shape[0]
    key_at = p * (rows - keys)
    query_at = p * (rows - queries)
    count = jnp.sum(valid[...])
    values = frames[pl.ds(pl.multiple_of(key_at, 8), keys), :].astype(jnp.float32)
    normed[...] = layer_normed(values, gain[...], bias[...]).astype(jnp.bfloat16)
    k_out[...] = dot(normed[...], w[1]).astype(jnp.bfloat16)
    v_out[...] = dot(normed[...], w[2]).astype(jnp.bfloat16)
    picked = normed[pl.ds(pl.multiple_of(p * (keys - queries), 16), queries), :]
    q_out[...] = dot(picked, w[0]).astype(jnp.bfloat16)
    key_pos = positions((queries, keys), 1, key_at)
    query_pos = positions((queries, keys), 0, query_at)
    allowed = (jnp.abs(key_pos - query_pos) <= CTX) & (key_pos < count)
    for head in range(q_out.shape[1] // HEAD_DIM):
        at = slice(head * HEAD_DIM, (head + 1) * HEAD_DIM)
        scores = dot_t(q_out[:, at], k_out[:, at]) * SCALE
        scores = jnp.where(allowed, scores, NEG)
        top = jnp.max(scores, axis=-1, keepdims=True)
        raised = jnp.exp2(scores - top)
        total = jnp.sum(raised, axis=-1, keepdims=True)
        top_out[head] = jnp.broadcast_to(top, (queries, HEAD_DIM))
        total_out[head] = jnp.broadcast_to(total, (queries, HEAD_DIM))
        acc_out[:, at] = dot(raised.astype(jnp.bfloat16), v_out[:, at])


def halo_kernel(halo, frames, gain, bias, *refs):
    (w_a, wo_a, q_a, k_a, v_a, top_a, total_a, acc_a) = refs[:8]
    (w_b, wo_b, q_b, k_b, v_b, top_b, total_b, acc_b) = refs[8:16]
    keep, send, normed, far_normed, q_halo, att = refs[16:]
    p = lax.axis_index("mp")
    last = lax.axis_size("tm") - 1
    tm = lax.axis_index("tm")
    rows, queries, keys = frames.shape[0], q_a.shape[0], k_a.shape[0]
    width = q_a.shape[1]
    present = jnp.where(p == 0, tm > 0, tm < last)
    near = halo[pl.ds(pl.multiple_of(EXT * (1 - p), 8), CTX), :].astype(jnp.float32)
    far = halo[pl.ds(pl.multiple_of(CTX * p, 8), EXT), :].astype(jnp.float32)
    values = layer_normed(jnp.concatenate([near, far], axis=0), gain[...], bias[...])
    far_normed[...] = values
    normed[...] = values.astype(jnp.bfloat16)
    ext_normed = far_normed[pl.ds(pl.multiple_of((CTX - EXT) * (1 - p), 8), EXT), :]
    ext_normed = ext_normed.astype(jnp.bfloat16)
    near_at = jnp.where(p == 0, -CTX, rows)
    far_at = jnp.where(p == 0, -HALO, rows + CTX)
    ext_at = jnp.where(p == 0, -EXT, rows)
    touched = p * (queries - CTX)
    query_pos = positions((CTX, CTX), 0, p * (rows - CTX))
    near_pos = positions((CTX, CTX), 1, near_at)
    allowed = (jnp.abs(near_pos - query_pos) <= CTX) & present
    own_at = p * (keys - CTX)
    ext_own = jnp.abs(positions((EXT, CTX), 1, p * (rows - CTX)) - positions((EXT, CTX), 0, ext_at)) <= CTX
    ext_near = jnp.abs(positions((EXT, CTX), 1, near_at) - positions((EXT, CTX), 0, ext_at)) <= CTX
    ext_far = jnp.abs(positions((EXT, EXT), 1, far_at) - positions((EXT, EXT), 0, ext_at)) <= CTX
    for side, (w, q, k, v, top_own, total_own, acc_own) in enumerate(
        ((w_a, q_a, k_a, v_a, top_a, total_a, acc_a), (w_b, q_b, k_b, v_b, top_b, total_b, acc_b))
    ):
        k_halo = dot(normed[...], w[1])
        v_halo = dot(normed[...], w[2])
        q_ext = dot(ext_normed, w[0])
        for head in range(width // HEAD_DIM):
            at = slice(head * HEAD_DIM, (head + 1) * HEAD_DIM)
            to = slice(side * width + at.start, side * width + at.stop)
            k_near = k_halo[:CTX, at].astype(jnp.bfloat16)
            v_near = v_halo[:CTX, at].astype(jnp.bfloat16)
            k_far = k_halo[CTX:, at].astype(jnp.bfloat16)
            v_far = v_halo[CTX:, at].astype(jnp.bfloat16)
            part = pl.ds(pl.multiple_of(touched, 8), CTX)
            scores = dot_t(q[part, at], k_near) * SCALE
            scores = jnp.where(allowed, scores, NEG)
            before = top_own[head, part, :]
            top = jnp.maximum(before, jnp.max(scores, axis=-1, keepdims=True))
            raised = jnp.exp2(scores - top)
            faded = jnp.exp2(before - top)
            total = total_own[head, part, :] * faded + jnp.sum(raised, axis=-1, keepdims=True)
            acc = acc_own[part, at] * faded + dot(raised.astype(jnp.bfloat16), v_near)
            att[:queries, to] = acc_own[:, at] / total_own[head]
            att[part, to] = acc / total
            q_head = q_ext[:, at].astype(jnp.bfloat16)
            own = pl.ds(pl.multiple_of(own_at, 8), CTX)
            s_own = jnp.where(ext_own, dot_t(q_head, k[own, at]) * SCALE, NEG)
            s_near = jnp.where(ext_near, dot_t(q_head, k_near) * SCALE, NEG)
            s_far = jnp.where(ext_far, dot_t(q_head, k_far) * SCALE, NEG)
            top = jnp.maximum(
                jnp.maximum(
                    jnp.max(s_own, axis=-1, keepdims=True), jnp.max(s_near, axis=-1, keepdims=True)
                ),
                jnp.max(s_far, axis=-1, keepdims=True),
            )
            r_own, r_near, r_far = jnp.exp2(s_own - top), jnp.exp2(s_near - top), jnp.exp2(s_far - top)
            total = (
                jnp.sum(r_own, axis=-1, keepdims=True)
                + jnp.sum(r_near, axis=-1, keepdims=True)
                + jnp.sum(r_far, axis=-1, keepdims=True)
            )
            acc = (
                dot(r_own.astype(jnp.bfloat16), v[own, at])
                + dot(r_near.astype(jnp.bfloat16), v_near)
                + dot(r_far.astype(jnp.bfloat16), v_far)
            )
            att[queries:, to] = acc / total
    attended = att[...].astype(jnp.bfloat16)
    here = pl.ds(pl.multiple_of(p * width, width), width)
    there = pl.ds(pl.multiple_of((1 - p) * width, width), width)
    own_rows = pl.ds(pl.multiple_of(p * (rows - queries), 8), queries)
    ext_rows = pl.ds(pl.multiple_of(CTX * (1 - p), 8), EXT)
    for wo, columns, out in ((wo_b, there, send), (wo_a, here, keep)):
        projected = dot(attended[:, :width], wo[here, :]) + dot(attended[:, width:], wo[there, :])
        out[:queries] = (frames[own_rows, columns].astype(jnp.float32) + projected[:queries]).astype(
            jnp.bfloat16
        )
        out[queries:] = (halo[ext_rows, columns].astype(jnp.float32) + projected[queries:]).astype(
            jnp.bfloat16
        )


def conv_kernel(keep, got, valid, weight, scale, shift, out, plain, masked):
    p = lax.axis_index("mp")
    tm = lax.axis_index("tm")
    last = lax.axis_size("tm") - 1
    rows = out.shape[0]
    half = rows // 2
    queries = keep.shape[0] - EXT
    count = jnp.sum(valid[...])

    def place(block, core):
        start = pl.ds(pl.multiple_of(core * (queries - half), 8), half)
        plain[pl.ds(pl.multiple_of(EXT + core * half, 8), half), :] = block[start, :].astype(
            jnp.float32
        )
        edge = block[queries:, :].astype(jnp.float32)
        inside = jnp.where(core == 0, tm > 0, tm < last)
        masked[pl.ds(pl.multiple_of(core * (EXT + rows), 8), EXT), :] = jnp.where(inside, edge, 0.0)

    place(keep, p)
    place(got, 1 - p)
    step = 32
    for at in range(0, rows, step):
        values = plain[EXT + at : EXT + at + step, :]
        row = positions(values.shape, 0, at)
        masked[EXT + at : EXT + at + step, :] = jnp.where(row < count, values, 0.0)
    for column in range(0, out.shape[1], 128):
        lanes = slice(column, column + 128)
        for at in range(0, rows, step):
            conv = jnp.zeros((step, 128), jnp.float32)
            for tap in range(KERNEL):
                begin = EXT - KERNEL // 2 + at + tap
                conv = conv + masked[begin : begin + step, lanes] * weight[tap : tap + 1, lanes]
            v = scale[:, lanes] * conv + shift[:, lanes]
            out[at : at + step, lanes] = (
                plain[EXT + at : EXT + at + step, lanes] + v / (1.0 + jnp.exp(-v))
            ).astype(jnp.bfloat16)


def local(frames, valid, norm_gain, norm_bias, w_qkv, w_out, conv_weight, conv_scale, conv_shift):
    rows, model = frames.shape
    width = w_qkv.shape[2]
    heads = width // HEAD_DIM
    count = lax.axis_size("tm")
    mp = lax.axis_index("mp")
    half = rows // 2
    queries = half + EXT
    keys = half + EXT + CTX
    assert rows >= HALO + CTX and rows % 16 == 0
    pairs = []
    for i in range(count - 1):
        pairs += [(2 * i, 2 * (i + 1)), (2 * (i + 1) + 1, 2 * i + 1)]
    other = [(0, 1), (1, 0)]
    sent = lax.dynamic_slice_in_dim(frames, (1 - mp) * (rows - HALO), HALO, 0)
    halo = lax.ppermute(sent, ("tm", "mp"), pairs)
    w_other = lax.ppermute(w_qkv, "mp", other)
    wo_other = lax.ppermute(w_out, "mp", other)
    valid = valid.reshape(1, rows)
    gain, bias = norm_gain.reshape(1, model), norm_bias.reshape(1, model)

    def own(w):
        f32, bf16 = jnp.float32, jnp.bfloat16
        return pl.pallas_call(
            own_kernel,
            out_shape=(
                jax.ShapeDtypeStruct((queries, width), bf16),
                jax.ShapeDtypeStruct((keys, width), bf16),
                jax.ShapeDtypeStruct((keys, width), bf16),
                jax.ShapeDtypeStruct((heads, queries, HEAD_DIM), f32),
                jax.ShapeDtypeStruct((heads, queries, HEAD_DIM), f32),
                jax.ShapeDtypeStruct((queries, width), f32),
            ),
            in_specs=[VMEM] * 5,
            out_specs=(VMEM,) * 6,
            scratch_shapes=[pltpu.VMEM((keys, model), bf16)],
            compiler_params=pltpu.CompilerParams(vmem_limit_bytes=20 << 20),
            cost_estimate=pl.CostEstimate(
                flops=2_000_000_000, bytes_accessed=4_000_000, transcendentals=300_000
            ),
            name="own",
        )(frames, valid, gain, bias, w)

    mine = own(w_qkv)
    theirs = own(w_other)
    keep, send = pl.pallas_call(
        halo_kernel,
        out_shape=(jax.ShapeDtypeStruct((queries + EXT, width), jnp.bfloat16),) * 2,
        in_specs=[VMEM] * 20,
        out_specs=(VMEM,) * 2,
        scratch_shapes=[
            pltpu.VMEM((HALO, model), jnp.bfloat16),
            pltpu.VMEM((HALO, model), jnp.float32),
            pltpu.VMEM((EXT, model), jnp.float32),
            pltpu.VMEM((queries + EXT, 2 * width), jnp.float32),
        ],
        compiler_params=pltpu.CompilerParams(vmem_limit_bytes=20 << 20),
        cost_estimate=pl.CostEstimate(
            flops=1_500_000_000, bytes_accessed=10_000_000, transcendentals=300_000
        ),
        name="halo",
    )(halo, frames, gain, bias, w_qkv, w_out, *mine, w_other, wo_other, *theirs)
    got = lax.ppermute(send, "mp", other)
    return pl.pallas_call(
        conv_kernel,
        out_shape=jax.ShapeDtypeStruct((rows, width), jnp.bfloat16),
        in_specs=[VMEM] * 6,
        out_specs=VMEM,
        scratch_shapes=[pltpu.VMEM((rows + 2 * EXT, width), jnp.float32)] * 2,
        compiler_params=pltpu.CompilerParams(vmem_limit_bytes=20 << 20),
        name="conv",
    )(keep, got, valid, conv_weight, conv_scale.reshape(1, width), conv_shift.reshape(1, width))


def solution(mesh):
    placed = (
        P("tm", None),
        P("tm"),
        P(),
        P(),
        P(None, None, "mp"),
        P(None, "mp"),
        P(None, "mp"),
        P("mp"),
        P("mp"),
    )
    return jax.shard_map(
        local, mesh=mesh, in_specs=placed, out_specs=P("tm", "mp"), check_vma=False
    )
```

```python
import math

import jax
import jax.numpy as jnp
from jax import lax
from jax.experimental import pallas as pl
from jax.experimental.pallas import tpu as pltpu
from jax.sharding import PartitionSpec as P

HEAD_DIM = 128
CTX = 128
KERNEL = 9
EXT = 8
HALO = CTX + EXT
PAD = 16
SPAN = CTX + PAD + CTX
NEG = -1e30
SCALE = math.log2(math.e) / math.sqrt(HEAD_DIM)
VMEM = pl.BlockSpec(memory_space=pltpu.VMEM)
ANY = pl.BlockSpec(memory_space=pl.ANY)
SMEM = pl.BlockSpec(memory_space=pltpu.SMEM)
F32, BF16 = jnp.float32, jnp.bfloat16


def layer_normed(values, gain, bias):
    center = values - jnp.mean(values, axis=-1, keepdims=True)
    spread = jnp.mean(center * center, axis=-1, keepdims=True)
    return center * lax.rsqrt(spread + 1e-05) * gain + bias


def dot(a, b):
    return jnp.dot(a, b, preferred_element_type=F32)


def dot_t(a, b):
    return lax.dot_general(a, b, (((1,), (1,)), ((), ())), preferred_element_type=F32)


def positions(shape, dim, start):
    return lax.broadcasted_iota(jnp.int32, shape, dim) + start


def rows_at(start, size):
    return pl.ds(pl.multiple_of(start, 8), size)


def pick_kernel(frames, sent):
    p = lax.axis_index("mp")
    sent[...] = frames[rows_at((1 - p) * (frames.shape[0] - HALO), HALO), :]


def own_heads(normed, w, count, q_out, k_out, v_out, top_out, total_out, acc_out, att_out):
    p = lax.axis_index("mp")
    keys, queries = k_out.shape[0], q_out.shape[0]
    rows = 2 * (queries - EXT)
    key_at, query_at = p * (rows - keys), p * (rows - queries)
    k_out[...] = dot(normed[...], w[1]).astype(BF16)
    picked = normed[pl.ds(pl.multiple_of(p * (keys - queries), 16), queries), :]
    q_out[...] = dot(picked, w[0]).astype(BF16)
    v_out[...] = dot(normed[...], w[2]).astype(BF16)
    key_pos = positions((queries, keys), 1, key_at)
    query_pos = positions((queries, keys), 0, query_at)
    allowed = (jnp.abs(key_pos - query_pos) <= CTX) & (key_pos < count)
    for head in range(q_out.shape[1] // HEAD_DIM):
        at = slice(head * HEAD_DIM, (head + 1) * HEAD_DIM)
        scores = dot_t(q_out[:, at], k_out[:, at]) * SCALE
        scores = jnp.where(allowed, scores, NEG)
        top = jnp.max(scores, axis=-1, keepdims=True)
        raised = jnp.exp2(scores - top)
        total = jnp.sum(raised, axis=-1, keepdims=True)
        top_out[head] = jnp.broadcast_to(top, (queries, HEAD_DIM))
        total_out[head] = jnp.broadcast_to(total, (queries, HEAD_DIM))
        acc = dot(raised.astype(BF16), v_out[:, at])
        acc_out[:, at] = acc
        att_out[:, at] = (acc * (1.0 / total)).astype(BF16)


def first_kernel(
    frames, valid, gain, bias, w, q, k, v, top, total, acc, att, normed, count_here
):
    p = lax.axis_index("mp")
    rows, keys = frames.shape[0], normed.shape[0]
    low, high = jnp.int32(0), jnp.int32(rows)
    for _ in range(rows.bit_length()):
        middle = (low + high) // 2
        one = valid[jnp.minimum(middle, rows - 1)] > 0
        open_ = low < high
        low = jnp.where(open_ & one, middle + 1, low)
        high = jnp.where(open_ & jnp.logical_not(one), middle, high)
    count = low
    count_here[...] = jnp.full(count_here.shape, count, jnp.int32)
    values = frames[rows_at(p * (rows - keys), keys), :].astype(F32)
    normed[...] = layer_normed(values, gain[...], bias[...]).astype(BF16)
    own_heads(normed, w, count, q, k, v, top, total, acc, att)


def shift_matrix(out, core, count):
    half = out.shape[0] // KERNEL
    width = out.shape[1]
    queries = width - EXT
    rows = 2 * half
    tm, last = lax.axis_index("tm"), lax.axis_size("tm") - 1
    column = positions((1, width), 1, 0)
    edge = jnp.where(core == 0, -EXT, rows)
    time = jnp.where(column < queries, column + core * (rows - queries), column - queries + edge)
    low = jnp.where(tm > 0, -EXT, 0)
    high = jnp.where(tm < last, rows + EXT, count[0:1, :width])
    time = jnp.where((time >= low) & (time < high), time, -rows)
    for tap in range(KERNEL):
        row = positions((half, width), 0, core * half + tap - KERNEL // 2)
        out[tap * half : (tap + 1) * half, :] = jnp.where(row == time, 1.0, 0.0).astype(BF16)


def second_kernel(
    normed, w, count_here, q, k, v, top, total, acc, att, own_shift, other_shift
):
    p = lax.axis_index("mp")
    keys = k.shape[0]
    count = jnp.concatenate([count_here[0:1, :]] * pl.cdiv(keys, count_here.shape[1]), axis=1)[:, :keys]
    own_heads(normed, w, count, q, k, v, top, total, acc, att)
    shift_matrix(own_shift, p, count_here)
    shift_matrix(other_shift, 1 - p, count_here)


def halo_kernel(halo, frames, gain, bias, wo_a, wo_b, *refs):
    parts = (refs[:8], refs[8:16])
    keep, send, normed, far_normed, kx, vx, att_all = refs[16:]
    p = lax.axis_index("mp")
    last = lax.axis_size("tm") - 1
    tm = lax.axis_index("tm")
    rows, queries, keys = frames.shape[0], refs[1].shape[0], refs[2].shape[0]
    width = refs[1].shape[1]
    heads = width // HEAD_DIM
    present = jnp.where(p == 0, tm > 0, tm < last)
    near = halo[rows_at(EXT * (1 - p), CTX), :].astype(F32)
    far = halo[rows_at(CTX * p, EXT), :].astype(F32)
    values = layer_normed(jnp.concatenate([near, far], axis=0), gain[...], bias[...])
    far_normed[...] = values
    normed[...] = values.astype(BF16)
    ext_normed = far_normed[rows_at((CTX - EXT) * (1 - p), EXT), :].astype(BF16)
    near_at = jnp.where(p == 0, -CTX, rows)
    far_at = jnp.where(p == 0, -HALO, rows + CTX)
    ext_at = jnp.where(p == 0, -EXT, rows)
    part = rows_at(p * (queries - CTX), CTX)
    own = rows_at(p * (keys - CTX), CTX)
    own_pos = p * (rows - CTX)
    blank = jnp.zeros((PAD - EXT, width), F32)
    q_ext = []
    for side, (w, q, k, v, top_own, total_own, acc_own, att) in enumerate(parts):
        to = slice(side * width, (side + 1) * width)
        kx[CTX + PAD :, to] = k[own, :]
        vx[CTX + PAD :, to] = v[own, :]
        att_all[:queries, to] = att[...]
    for side, (w, q, k, v, top_own, total_own, acc_own, att) in enumerate(parts):
        to = slice(side * width, (side + 1) * width)
        for x, i in ((kx, 1), (vx, 2)):
            got = dot(normed[...], w[i])
            x[:CTX, to] = got[:CTX].astype(BF16)
            x[CTX : CTX + PAD, to] = jnp.concatenate([got[CTX:], blank], axis=0).astype(BF16)
        q_ext.append(dot(ext_normed, w[0]))
    q_ext = jnp.concatenate(q_ext, axis=1)
    deep = 2 * heads * EXT
    tiled = jnp.concatenate([q_ext] * (2 * heads), axis=0)
    head_of_row = positions(tiled.shape, 0, 0) // EXT
    head_of_lane = positions(tiled.shape, 1, 0) // HEAD_DIM
    tiled = jnp.where(head_of_row == head_of_lane, tiled, 0.0).astype(BF16)
    column = positions((deep, SPAN), 1, 0)
    key_pos = jnp.where(
        column < CTX,
        column + near_at,
        jnp.where(column < CTX + EXT, column - CTX + far_at, column - (CTX + PAD) + own_pos),
    )
    row_pos = positions((deep, SPAN), 0, 0) % EXT + ext_at
    seen = (jnp.abs(key_pos - row_pos) <= CTX) & ((column < CTX + EXT) | (column >= CTX + PAD))
    scores = jnp.where(seen, dot_t(tiled, kx[...]) * SCALE, NEG)
    top = jnp.max(scores, axis=-1, keepdims=True)
    raised = jnp.exp2(scores - top)
    total = jnp.sum(raised, axis=-1, keepdims=True)
    spread = dot(raised.astype(BF16), vx[...]) * (1.0 / total)
    ext_att = jnp.concatenate(
        [
            spread[h * EXT : (h + 1) * EXT, h * HEAD_DIM : (h + 1) * HEAD_DIM]
            for h in range(2 * heads)
        ],
        axis=1,
    )
    query_pos = positions((CTX, CTX), 0, p * (rows - CTX))
    near_pos = positions((CTX, CTX), 1, near_at)
    allowed = (jnp.abs(near_pos - query_pos) <= CTX) & present
    for side, (w, q, k, v, top_own, total_own, acc_own, att) in enumerate(parts):
        for head in range(heads):
            at = slice(head * HEAD_DIM, (head + 1) * HEAD_DIM)
            to = slice(side * width + at.start, side * width + at.stop)
            scores = dot_t(q[part, at], kx[:CTX, to]) * SCALE
            scores = jnp.where(allowed, scores, NEG)
            before = top_own[head, part, :]
            top = jnp.maximum(before, jnp.max(scores, axis=-1, keepdims=True))
            raised = jnp.exp2(scores - top)
            faded = jnp.exp2(before - top)
            total = total_own[head, part, :] * faded + jnp.sum(raised, axis=-1, keepdims=True)
            acc = acc_own[part, at] * faded + dot(raised.astype(BF16), vx[:CTX, to])
            att_all[part, to] = (acc / total).astype(BF16)
    ext_att = jnp.concatenate([ext_att, jnp.zeros_like(ext_att)], axis=0).astype(BF16)
    here = pl.ds(pl.multiple_of(p * width, width), width)
    there = pl.ds(pl.multiple_of((1 - p) * width, width), width)
    own_rows = rows_at(p * (rows - queries), queries)
    ext_rows = rows_at(CTX * (1 - p), EXT)
    for wo, columns, out in ((wo_b, there, send), (wo_a, here, keep)):
        projected = dot(att_all[:, :width], wo[here, :]) + dot(att_all[:, width:], wo[there, :])
        out[:queries] = (frames[own_rows, columns].astype(F32) + projected).astype(BF16)
        edge = dot(ext_att[:, :width], wo[here, :]) + dot(ext_att[:, width:], wo[there, :])
        out[queries:] = (halo[ext_rows, columns].astype(F32) + edge[:EXT]).astype(BF16)


def convolved(block, core, shift_by, weight, scale, shift, store):
    half = shift_by.shape[0] // KERNEL
    queries = block.shape[0] - EXT
    rows = rows_at(core * (queries - half), half)
    step = 256
    for at in range(0, block.shape[1], step):
        lanes = slice(at, at + step)
        gain = 0.5 * scale[:, lanes]
        u = jnp.broadcast_to(0.5 * shift[:, lanes], (half, step))
        for tap in range(KERNEL):
            moved = dot(shift_by[tap * half : (tap + 1) * half, :], block[:, lanes])
            u = u + moved * (weight[tap : tap + 1, lanes] * gain)
        plain = block[rows, lanes].astype(F32)
        store(lanes, (plain + (u + u * jnp.tanh(u))).astype(BF16))


def own_conv_kernel(keep, shift_by, weight, scale, shift, out):
    def store(lanes, value):
        out[:, lanes] = value

    convolved(keep, lax.axis_index("mp"), shift_by, weight, scale, shift, store)


def other_conv_kernel(got, done, shift_by, weight, scale, shift, out, block, sems):
    core = 1 - lax.axis_index("mp")
    half = done.shape[0]
    first = pltpu.make_async_copy(done, out.at[rows_at((1 - core) * half, half), :], sems.at[0])
    first.start()
    copies = [first]

    def store(lanes, value):
        block[:, lanes] = value
        copies.append(
            pltpu.make_async_copy(
                block.at[:, lanes], out.at[rows_at(core * half, half), lanes], sems.at[len(copies)]
            )
        )
        copies[-1].start()

    convolved(got, core, shift_by, weight, scale, shift, store)
    for copy in copies:
        copy.wait()


def call(kernel, name, out_shape, in_specs, out_specs, scratch=(), flops=0, size=0, exps=0, limit=16):
    return pl.pallas_call(
        kernel,
        out_shape=out_shape,
        in_specs=in_specs,
        out_specs=out_specs,
        scratch_shapes=scratch,
        compiler_params=pltpu.CompilerParams(vmem_limit_bytes=limit << 20),
        cost_estimate=pl.CostEstimate(flops=flops, bytes_accessed=size, transcendentals=exps),
        name=name,
    )


def local(frames, valid, norm_gain, norm_bias, w_qkv, w_out, conv_weight, conv_scale, conv_shift):
    rows, model = frames.shape
    width = w_qkv.shape[2]
    heads = width // HEAD_DIM
    count = lax.axis_size("tm")
    half = rows // 2
    queries = half + EXT
    keys = half + EXT + CTX
    block = queries + EXT
    assert rows >= HALO + CTX and rows % 32 == 0
    shaped = jax.ShapeDtypeStruct
    pairs = []
    for i in range(count - 1):
        pairs += [(2 * i, 2 * (i + 1)), (2 * (i + 1) + 1, 2 * i + 1)]
    other = [(0, 1), (1, 0)]
    sent = call(
        pick_kernel, "pick", shaped((HALO, model), BF16), [VMEM], VMEM, flops=5_000_000_000
    )(frames)
    halo = lax.ppermute(sent, ("tm", "mp"), pairs)
    w_other = lax.ppermute(w_qkv, "mp", other)
    wo_other = lax.ppermute(w_out, "mp", other)
    gain, bias = norm_gain.reshape(1, model), norm_bias.reshape(1, model)
    results = (
        shaped((queries, width), BF16),
        shaped((keys, width), BF16),
        shaped((keys, width), BF16),
        shaped((heads, queries, HEAD_DIM), F32),
        shaped((heads, queries, HEAD_DIM), F32),
        shaped((queries, width), F32),
        shaped((queries, width), BF16),
    )
    first = call(
        first_kernel,
        "first",
        results + (shaped((keys, model), BF16), shaped((8, 256), jnp.int32)),
        [VMEM, SMEM, VMEM, VMEM, VMEM],
        (VMEM,) * 9,
        flops=1_300_000_000,
        size=4_000_000,
        exps=300_000,
    )(frames, valid, gain, bias, w_qkv)
    mine, (normed, count_here) = first[:7], first[7:]
    second = call(
        second_kernel,
        "second",
        results + (shaped((KERNEL * half, block), BF16),) * 2,
        [VMEM] * 3,
        (VMEM,) * 9,
        flops=1_300_000_000,
        size=4_000_000,
        exps=300_000,
    )(normed, w_other, count_here)
    theirs, (own_shift, other_shift) = second[:7], second[7:]
    keep, send = call(
        halo_kernel,
        "halo",
        (shaped((block, width), BF16),) * 2,
        [VMEM] * 22,
        (VMEM,) * 2,
        [
            pltpu.VMEM((HALO, model), BF16),
            pltpu.VMEM((HALO, model), F32),
            pltpu.VMEM((SPAN, model), BF16),
            pltpu.VMEM((SPAN, model), BF16),
            pltpu.VMEM((queries, model), BF16),
        ],
        flops=1_500_000_000,
        size=10_000_000,
        exps=300_000,
    )(halo, frames, gain, bias, w_out, wo_other, w_qkv, *mine, w_other, *theirs)
    got = lax.ppermute(send, "mp", other)
    weights = (conv_weight, conv_scale.reshape(1, width), conv_shift.reshape(1, width))
    done = call(
        own_conv_kernel,
        "own_conv",
        shaped((half, width), BF16),
        [VMEM] * 5,
        VMEM,
        flops=270_000_000,
        size=1_000_000,
    )(keep, own_shift, *weights)
    return call(
        other_conv_kernel,
        "other_conv",
        shaped((rows, width), BF16),
        [VMEM] * 6,
        ANY,
        [pltpu.VMEM((half, width), BF16), pltpu.SemaphoreType.DMA((1 + width // 256,))],
        flops=270_000_000,
        size=1_000_000,
    )(got, done, other_shift, *weights)


def solution(mesh):
    placed = (
        P("tm", None),
        P("tm"),
        P(),
        P(),
        P(None, None, "mp"),
        P(None, "mp"),
        P(None, "mp"),
        P("mp"),
        P("mp"),
    )
    return jax.shard_map(
        local, mesh=mesh, in_specs=placed, out_specs=P("tm", "mp"), check_vma=False
    )
```

```python
import math

import jax
import jax.numpy as jnp
from jax import lax
from jax.experimental import pallas as pl
from jax.experimental.pallas import tpu as pltpu
from jax.sharding import PartitionSpec as P

HEAD_DIM = 128
CTX = 128
KERNEL = 9
EXT = 8
HALO = CTX + EXT
PAD = 16
SPAN = CTX + PAD + CTX
NEG = -1e30
WARM_FLOPS, PICK_FLOPS, NORM_FLOPS = 1_500_000_000, 1_000_000_000, 1_500_000_000
SCALE = math.log2(math.e) / math.sqrt(HEAD_DIM)
VMEM = pl.BlockSpec(memory_space=pltpu.VMEM)
ANY = pl.BlockSpec(memory_space=pl.ANY)
SMEM = pl.BlockSpec(memory_space=pltpu.SMEM)
F32, BF16 = jnp.float32, jnp.bfloat16


def layer_normed(values, gain, bias):
    center = values - jnp.mean(values, axis=-1, keepdims=True)
    spread = jnp.mean(center * center, axis=-1, keepdims=True)
    return center * lax.rsqrt(spread + 1e-05) * gain + bias


def norm_rows(source, source_at, target, target_at, count, gain, bias):
    step = 16
    for at in range(0, count, step):
        size = min(step, count - at)
        values = source[rows_at(source_at + at, size), :].astype(F32)
        target[target_at + at : target_at + at + size, :] = layer_normed(
            values, gain, bias
        ).astype(BF16)


def dot(a, b):
    return jnp.dot(a, b, preferred_element_type=F32)


def dot_t(a, b):
    return lax.dot_general(a, b, (((1,), (1,)), ((), ())), preferred_element_type=F32)


def positions(shape, dim, start):
    return lax.broadcasted_iota(jnp.int32, shape, dim) + start


def rows_at(start, size):
    return pl.ds(pl.multiple_of(start, 8), size)


def pick_kernel(frames, after, sent):
    p = lax.axis_index("mp")
    sent[...] = frames[rows_at((1 - p) * (frames.shape[0] - HALO), HALO), :]


def own_heads(normed, w, count, q_out, k_out, v_out, top_out, total_out, acc_out, att_out):
    p = lax.axis_index("mp")
    keys, queries = k_out.shape[0], q_out.shape[0]
    rows = 2 * (queries - EXT)
    key_at, query_at = p * (rows - keys), p * (rows - queries)
    k_out[...] = dot(normed[...], w[1]).astype(BF16)
    picked = normed[pl.ds(pl.multiple_of(p * (keys - queries), 16), queries), :]
    q_out[...] = (dot(picked, w[0]) * SCALE).astype(BF16)
    v_out[...] = dot(normed[...], w[2]).astype(BF16)
    key_pos = positions((queries, keys), 1, key_at)
    query_pos = positions((queries, keys), 0, query_at)
    allowed = (jnp.abs(key_pos - query_pos) <= CTX) & (key_pos < count)
    for head in range(q_out.shape[1] // HEAD_DIM):
        at = slice(head * HEAD_DIM, (head + 1) * HEAD_DIM)
        scores = dot_t(q_out[:, at], k_out[:, at])
        scores = jnp.where(allowed, scores, NEG)
        top = jnp.max(scores, axis=-1, keepdims=True)
        raised = jnp.exp2(scores - top)
        total = jnp.sum(raised, axis=-1, keepdims=True)
        top_out[head] = jnp.broadcast_to(top, (queries, HEAD_DIM))
        total_out[head] = jnp.broadcast_to(total, (queries, HEAD_DIM))
        acc = dot(raised.astype(BF16), v_out[:, at])
        acc_out[:, at] = acc
        att_out[:, at] = (acc * (1.0 / total)).astype(BF16)


def norm_kernel(frames, valid, gain, bias, normed, count_here):
    p = lax.axis_index("mp")
    rows, keys = frames.shape[0], normed.shape[0]
    low, high = jnp.int32(0), jnp.int32(rows)
    for _ in range(rows.bit_length()):
        middle = (low + high) // 2
        one = valid[jnp.minimum(middle, rows - 1)] > 0
        open_ = low < high
        low = jnp.where(open_ & one, middle + 1, low)
        high = jnp.where(open_ & jnp.logical_not(one), middle, high)
    count_here[...] = jnp.full(count_here.shape, low, jnp.int32)
    norm_rows(frames, p * (rows - keys), normed, 0, keys, gain[...], bias[...])


def first_kernel(normed, w, count_here, q, k, v, top, total, acc, att):
    keys = k.shape[0]
    count = jnp.concatenate([count_here[0:1, :]] * pl.cdiv(keys, count_here.shape[1]), axis=1)[:, :keys]
    own_heads(normed, w, count, q, k, v, top, total, acc, att)


def warm_kernel(own_shift, other_shift):
    p = lax.axis_index("mp")
    for out, core in ((own_shift, p), (other_shift, 1 - p)):
        half, width = out.shape[0] // KERNEL, out.shape[1]
        queries, rows = width - EXT, 2 * half
        column = positions((1, width), 1, 0)
        edge = jnp.where(core == 0, -EXT, rows)
        time = jnp.where(column < queries, column + core * (rows - queries), column - queries + edge)
        for tap in range(KERNEL):
            row = positions((half, width), 0, core * half + tap - KERNEL // 2)
            out[tap * half : (tap + 1) * half, :] = jnp.where(row == time, 1.0, 0.0).astype(BF16)


def mask_shift(shift, core, count, out):
    half, width = out.shape[0] // KERNEL, out.shape[1]
    queries, rows = width - EXT, 2 * half
    tm, last = lax.axis_index("tm"), lax.axis_size("tm") - 1
    column = positions((1, width), 1, 0)
    edge = jnp.where(core == 0, -EXT, rows)
    time = jnp.where(column < queries, column + core * (rows - queries), column - queries + edge)
    low = jnp.where(tm > 0, -EXT, 0)
    high = jnp.where(tm < last, rows + EXT, count[0:1, :width])
    mask = jnp.where((time >= low) & (time < high), 1.0, 0.0).astype(BF16)
    for tap in range(KERNEL):
        at = slice(tap * half, (tap + 1) * half)
        out[at, :] = shift[at, :] * mask


def second_kernel(
    normed, w, count_here, own_base, other_base, q, k, v, top, total, acc, att, own_shift, other_shift
):
    p = lax.axis_index("mp")
    first_kernel(normed, w, count_here, q, k, v, top, total, acc, att)
    mask_shift(own_base, p, count_here, own_shift)
    mask_shift(other_base, 1 - p, count_here, other_shift)


def halo_kernel(halo, frames, gain, bias, wo, *refs):
    parts = (refs[:8], refs[8:16])
    send, att_all, normed, kx, vx = refs[16:]
    p = lax.axis_index("mp")
    last = lax.axis_size("tm") - 1
    tm = lax.axis_index("tm")
    rows, queries, keys = frames.shape[0], refs[1].shape[0], refs[2].shape[0]
    width = refs[1].shape[1]
    heads = width // HEAD_DIM
    present = jnp.where(p == 0, tm > 0, tm < last)
    norms = (gain[...], bias[...])
    ext_normed = layer_normed(halo[rows_at(CTX * (1 - p), EXT), :].astype(F32), *norms).astype(BF16)
    norm_rows(halo, EXT * (1 - p), normed, 0, CTX, *norms)
    norm_rows(halo, CTX * p, normed, CTX, EXT, *norms)
    near_at = jnp.where(p == 0, -CTX, rows)
    far_at = jnp.where(p == 0, -HALO, rows + CTX)
    ext_at = jnp.where(p == 0, -EXT, rows)
    part = rows_at(p * (queries - CTX), CTX)
    own = rows_at(p * (keys - CTX), CTX)
    own_pos = p * (rows - CTX)
    blank = jnp.zeros((PAD - EXT, width), F32)
    query_pos = positions((CTX, CTX), 0, p * (rows - CTX))
    near_pos = positions((CTX, CTX), 1, near_at)
    allowed = (jnp.abs(near_pos - query_pos) <= CTX) & present
    each = [
        (side, head, slice(head * HEAD_DIM, (head + 1) * HEAD_DIM))
        for side in range(2)
        for head in range(heads)
    ]

    def lanes_of(side, at):
        return slice(side * width + at.start, side * width + at.stop)

    for side, (w, q, k, v, top_own, total_own, acc_own, att) in enumerate(parts):
        to = slice(side * width, (side + 1) * width)
        kx[CTX + PAD :, to] = k[own, :]
        vx[CTX + PAD :, to] = v[own, :]
        att_all[:queries, to] = att[...]

    def project(x, i):
        for side, (w, *_) in enumerate(parts):
            to = slice(side * width, (side + 1) * width)
            got = dot(normed[...], w[i])
            x[:CTX, to] = got[:CTX].astype(BF16)
            x[CTX : CTX + PAD, to] = jnp.concatenate([got[CTX:], blank], axis=0).astype(BF16)

    q_ext = jnp.concatenate([dot(ext_normed, w[0]) * SCALE for w, *_ in parts], axis=1)
    project(kx, 1)
    deep = 2 * heads * EXT
    tiled = jnp.concatenate([q_ext] * (2 * heads), axis=0)
    head_of_row = positions(tiled.shape, 0, 0) // EXT
    head_of_lane = positions(tiled.shape, 1, 0) // HEAD_DIM
    tiled = jnp.where(head_of_row == head_of_lane, tiled, 0.0).astype(BF16)
    scores = [
        dot_t(parts[side][1][part, at], kx[:CTX, lanes_of(side, at)]) for side, head, at in each
    ]
    ext_scores = dot_t(tiled, kx[...])
    project(vx, 2)
    raised, total, faded = [], [], []
    for (side, head, at), score in zip(each, scores):
        top_own, total_own = parts[side][4], parts[side][5]
        score = jnp.where(allowed, score, NEG)
        before = top_own[head, part, :]
        top = jnp.maximum(before, jnp.max(score, axis=-1, keepdims=True))
        up = jnp.exp2(score - top)
        faded.append(jnp.exp2(before - top))
        total.append(
            total_own[head, part, :] * faded[-1] + jnp.sum(up, axis=-1, keepdims=True)
        )
        raised.append(up.astype(BF16))
    column = positions((deep, SPAN), 1, 0)
    key_pos = jnp.where(
        column < CTX,
        column + near_at,
        jnp.where(column < CTX + EXT, column - CTX + far_at, column - (CTX + PAD) + own_pos),
    )
    row_pos = positions((deep, SPAN), 0, 0) % EXT + ext_at
    seen = (jnp.abs(key_pos - row_pos) <= CTX) & ((column < CTX + EXT) | (column >= CTX + PAD))
    ext_scores = jnp.where(seen, ext_scores, NEG)
    ext_up = jnp.exp2(ext_scores - jnp.max(ext_scores, axis=-1, keepdims=True))
    ext_total = jnp.sum(ext_up, axis=-1, keepdims=True)
    gathered = [
        dot(up, vx[:CTX, lanes_of(side, at)]) for (side, head, at), up in zip(each, raised)
    ]
    spread = dot(ext_up.astype(BF16), vx[...]) * (1.0 / ext_total)
    for i, (side, head, at) in enumerate(each):
        acc = parts[side][6][part, at] * faded[i] + gathered[i]
        att_all[part, lanes_of(side, at)] = (acc / total[i]).astype(BF16)
    ext_att = jnp.concatenate(
        [
            spread[h * EXT : (h + 1) * EXT, h * HEAD_DIM : (h + 1) * HEAD_DIM]
            for h in range(2 * heads)
        ],
        axis=1,
    )
    tail = att_all.shape[0] - PAD
    att_all[tail:, :] = jnp.concatenate([ext_att, jnp.zeros_like(ext_att)], axis=0).astype(BF16)
    mix(att_all, frames, halo, wo, 1 - p, send)


def mix(att_all, frames, halo, wo, columns, out):
    p = lax.axis_index("mp")
    rows, width = frames.shape[0], out.shape[1]
    queries, tail = out.shape[0] - EXT, att_all.shape[0] - PAD
    here = pl.ds(pl.multiple_of(p * width, width), width)
    there = pl.ds(pl.multiple_of((1 - p) * width, width), width)
    lanes = pl.ds(pl.multiple_of(columns * width, width), width)
    projected = dot(att_all[:, :width], wo[here, :]) + dot(att_all[:, width:], wo[there, :])
    own = frames[rows_at(p * (rows - queries), queries), lanes].astype(F32)
    out[:queries] = (own + projected[:queries]).astype(BF16)
    edge = halo[rows_at(CTX * (1 - p), EXT), lanes].astype(F32)
    out[queries:] = (edge + projected[tail : tail + EXT]).astype(BF16)


def keep_kernel(att_all, frames, halo, wo, keep):
    mix(att_all, frames, halo, wo, lax.axis_index("mp"), keep)


def convolved(block, core, shift_by, weight, scale, shift, store):
    half = shift_by.shape[0] // KERNEL
    queries = block.shape[0] - EXT
    rows = rows_at(core * (queries - half), half)
    step = 256
    for at in range(0, block.shape[1], step):
        lanes = slice(at, at + step)
        gain = 0.5 * scale[:, lanes]
        u = jnp.broadcast_to(0.5 * shift[:, lanes], (half, step))
        for tap in range(KERNEL):
            moved = dot(shift_by[tap * half : (tap + 1) * half, :], block[:, lanes])
            u = u + moved * (weight[tap : tap + 1, lanes] * gain)
        plain = block[rows, lanes].astype(F32)
        store(lanes, (plain + (u + u * jnp.tanh(u))).astype(BF16))


def own_conv_kernel(keep, shift_by, weight, scale, shift, out):
    def store(lanes, value):
        out[:, lanes] = value

    convolved(keep, lax.axis_index("mp"), shift_by, weight, scale, shift, store)


def other_conv_kernel(got, done, shift_by, weight, scale, shift, out, block, sems):
    core = 1 - lax.axis_index("mp")
    half = done.shape[0]
    first = pltpu.make_async_copy(done, out.at[rows_at((1 - core) * half, half), :], sems.at[0])
    first.start()
    copies = [first]

    def store(lanes, value):
        block[:, lanes] = value
        copies.append(
            pltpu.make_async_copy(
                block.at[:, lanes], out.at[rows_at(core * half, half), lanes], sems.at[len(copies)]
            )
        )
        copies[-1].start()

    convolved(got, core, shift_by, weight, scale, shift, store)
    for copy in copies:
        copy.wait()


def call(kernel, out_shape, in_specs, out_specs, scratch=(), flops=0, size=0, exps=0, limit=16):
    return pl.pallas_call(
        kernel,
        out_shape=out_shape,
        in_specs=in_specs,
        out_specs=out_specs,
        scratch_shapes=scratch,
        compiler_params=pltpu.CompilerParams(vmem_limit_bytes=limit << 20),
        cost_estimate=pl.CostEstimate(flops=flops, bytes_accessed=size, transcendentals=exps),
    )


def compute(frames, valid, norm_gain, norm_bias, w_qkv, w_out, conv_weight, conv_scale, conv_shift):
    rows, model = frames.shape
    width = w_qkv.shape[2]
    heads = width // HEAD_DIM
    count = lax.axis_size("tm")
    half = rows // 2
    queries = half + EXT
    keys = half + EXT + CTX
    block = queries + EXT
    assert rows >= HALO + CTX and rows % 32 == 0
    shaped = jax.ShapeDtypeStruct
    pairs = []
    for i in range(count - 1):
        pairs += [(2 * i, 2 * (i + 1)), (2 * (i + 1) + 1, 2 * i + 1)]
    other = [(0, 1), (1, 0)]
    shift_shapes = (shaped((KERNEL * half, block), BF16),) * 2
    shifts = call(warm_kernel, shift_shapes, [], (VMEM,) * 2, flops=WARM_FLOPS)()
    sent = call(
        pick_kernel, shaped((HALO, model), BF16), [VMEM, ANY], VMEM, flops=PICK_FLOPS
    )(frames, shifts[0])
    halo = lax.ppermute(sent, ("tm", "mp"), pairs)
    w_other = lax.ppermute(w_qkv, "mp", other)
    wo_other = lax.ppermute(w_out, "mp", other)
    gain, bias = norm_gain.reshape(1, model), norm_bias.reshape(1, model)
    results = (
        shaped((queries, width), BF16),
        shaped((keys, width), BF16),
        shaped((keys, width), BF16),
        shaped((heads, queries, HEAD_DIM), F32),
        shaped((heads, queries, HEAD_DIM), F32),
        shaped((queries, width), F32),
        shaped((queries, width), BF16),
    )
    normed, count_here = call(
        norm_kernel,
        (shaped((keys, model), BF16), shaped((8, 256), jnp.int32)),
        [VMEM, SMEM, VMEM, VMEM],
        (VMEM,) * 2,
        flops=NORM_FLOPS,
        size=1_000_000,
    )(frames, valid, gain, bias)
    mine = call(
        first_kernel,
        results,
        [VMEM] * 3,
        (VMEM,) * 7,
        flops=1_300_000_000,
        size=4_000_000,
        exps=300_000,
    )(normed, w_qkv, count_here)
    second = call(
        second_kernel,
        results + shift_shapes,
        [VMEM] * 5,
        (VMEM,) * 9,
        flops=1_300_000_000,
        size=4_000_000,
        exps=300_000,
    )(normed, w_other, count_here, *shifts)
    theirs, (own_shift, other_shift) = second[:7], second[7:]
    send, att_all = call(
        halo_kernel,
        (shaped((block, width), BF16), shaped((pl.cdiv(queries, 16) * 16 + PAD, model), BF16)),
        [VMEM] * 21,
        (VMEM,) * 2,
        [
            pltpu.VMEM((HALO, model), BF16),
            pltpu.VMEM((SPAN, model), BF16),
            pltpu.VMEM((SPAN, model), BF16),
        ],
        flops=1_500_000_000,
        size=10_000_000,
        exps=300_000,
    )(halo, frames, gain, bias, wo_other, w_qkv, *mine, w_other, *theirs)
    got = lax.ppermute(send, "mp", other)
    keep = call(
        keep_kernel,
        shaped((block, width), BF16),
        [VMEM] * 4,
        VMEM,
        flops=200_000_000,
        size=1_000_000,
    )(att_all, frames, halo, w_out)
    weights = (conv_weight, conv_scale.reshape(1, width), conv_shift.reshape(1, width))
    done = call(
        own_conv_kernel,
        shaped((half, width), BF16),
        [VMEM] * 5,
        VMEM,
        flops=270_000_000,
        size=1_000_000,
    )(keep, own_shift, *weights)
    return call(
        other_conv_kernel,
        shaped((rows, width), BF16),
        [VMEM] * 6,
        ANY,
        [pltpu.VMEM((half, width), BF16), pltpu.SemaphoreType.DMA((1 + width // 256,))],
        flops=270_000_000,
        size=1_000_000,
    )(got, done, other_shift, *weights)


def solution(mesh):
    placed = (
        P("tm", None),
        P("tm"),
        P(),
        P(),
        P(None, None, "mp"),
        P(None, "mp"),
        P(None, "mp"),
        P("mp"),
        P("mp"),
    )
    return jax.shard_map(
        compute, mesh=mesh, in_specs=placed, out_specs=P("tm", "mp"), check_vma=False
    )
```

```python
import math

import jax
import jax.numpy as jnp
from jax import lax
from jax.experimental import pallas as pl
from jax.experimental.pallas import tpu as pltpu
from jax.sharding import PartitionSpec as P

HEAD_DIM = 128
CTX = 128
KERNEL = 9
EXT = 8
HALO = CTX + EXT
FAR = KERNEL // 2
LANES = 128
MIDDLE = KERNEL // 2
MOVED = [tap for tap in range(KERNEL) if tap != MIDDLE]
PAD = 16
SPAN = CTX + PAD + CTX
NEG = -1e30
GROUP = 2
WARM_FLOPS, PICK_FLOPS, NORM_FLOPS = 1_500_000_000, 1_000_000_000, 1_500_000_000
SCALE = math.log2(math.e) / math.sqrt(HEAD_DIM)
VMEM = pl.BlockSpec(memory_space=pltpu.VMEM)
ANY = pl.BlockSpec(memory_space=pl.ANY)
SMEM = pl.BlockSpec(memory_space=pltpu.SMEM)
F32, BF16 = jnp.float32, jnp.bfloat16


def layer_normed(values, gain, bias):
    center = values - jnp.mean(values, axis=-1, keepdims=True)
    spread = jnp.mean(center * center, axis=-1, keepdims=True)
    return center * lax.rsqrt(spread + 1e-05) * gain + bias


def norm_rows(source, source_at, target, target_at, count, gain, bias):
    step = 16
    for at in range(0, count, step):
        size = min(step, count - at)
        values = source[rows_at(source_at + at, size), :].astype(F32)
        target[target_at + at : target_at + at + size, :] = layer_normed(
            values, gain, bias
        ).astype(BF16)


def dot(a, b):
    return jnp.dot(a, b, preferred_element_type=F32)


def dot_t(a, b):
    return lax.dot_general(a, b, (((1,), (1,)), ((), ())), preferred_element_type=F32)


def positions(shape, dim, start):
    return lax.broadcasted_iota(jnp.int32, shape, dim) + start


def rows_at(start, size):
    return pl.ds(pl.multiple_of(start, 8), size)


def lane_blocks(width):
    return [slice(at, at + LANES) for at in range(0, width, LANES)]


def pick_kernel(frames, after, sent):
    p = lax.axis_index("mp")
    rows, width = frames.shape
    blocks = lane_blocks(width)
    near = rows_at((1 - p) * (rows - CTX), CTX)
    for i, lanes in enumerate(blocks):
        sent[i * CTX : (i + 1) * CTX, :] = frames[near, lanes]
    far = frames[rows_at((1 - p) * (rows - HALO) + p * CTX, EXT), :].astype(F32)
    far = jnp.where(p == 0, pltpu.roll(far, EXT - FAR, 0), far)
    sent[len(blocks) * CTX :, :] = jnp.concatenate(
        [far[:FAR, lanes] for lanes in blocks], axis=0
    ).astype(BF16)


def halo_rows(halo, start, size, blocks):
    return jnp.concatenate(
        [halo[rows_at(i * CTX + start, size), :].astype(F32) for i in blocks], axis=1
    )


def own_heads(normed, w, count, q_out, k_out, v_out, top_out, total_out, acc_out, att_out):
    p = lax.axis_index("mp")
    keys, queries = k_out.shape[0], q_out.shape[0]
    rows = 2 * (queries - EXT)
    key_at, query_at = p * (rows - keys), p * (rows - queries)
    k_out[...] = dot(normed[...], w[1]).astype(BF16)
    picked = normed[pl.ds(pl.multiple_of(p * (keys - queries), 16), queries), :]
    q_out[...] = (dot(picked, w[0]) * SCALE).astype(BF16)
    v_out[...] = dot(normed[...], w[2]).astype(BF16)
    key_pos = positions((queries, keys), 1, key_at)
    query_pos = positions((queries, keys), 0, query_at)
    allowed = (jnp.abs(key_pos - query_pos) <= CTX) & (key_pos < count)
    for head in range(q_out.shape[1] // HEAD_DIM):
        at = slice(head * HEAD_DIM, (head + 1) * HEAD_DIM)
        scores = dot_t(q_out[:, at], k_out[:, at])
        scores = jnp.where(allowed, scores, NEG)
        top = jnp.max(scores, axis=-1, keepdims=True)
        raised = jnp.exp2(scores - top)
        total = jnp.sum(raised, axis=-1, keepdims=True)
        top_out[head] = jnp.broadcast_to(top, (queries, HEAD_DIM))
        total_out[head] = jnp.broadcast_to(total, (queries, HEAD_DIM))
        acc = dot(raised.astype(BF16), v_out[:, at])
        acc_out[:, at] = acc
        att_out[:, at] = (acc * (1.0 / total)).astype(BF16)


def norm_kernel(frames, valid, gain, bias, normed, count_here):
    p = lax.axis_index("mp")
    rows, keys = frames.shape[0], normed.shape[0]
    low, high = jnp.int32(0), jnp.int32(rows)
    for _ in range(rows.bit_length()):
        middle = (low + high) // 2
        one = valid[jnp.minimum(middle, rows - 1)] > 0
        open_ = low < high
        low = jnp.where(open_ & one, middle + 1, low)
        high = jnp.where(open_ & jnp.logical_not(one), middle, high)
    count_here[...] = jnp.full(count_here.shape, low, jnp.int32)
    norm_rows(frames, p * (rows - keys), normed, 0, keys, gain[...], bias[...])


def first_kernel(normed, w, count_here, q, k, v, top, total, acc, att):
    keys = k.shape[0]
    count = jnp.concatenate([count_here[0:1, :]] * pl.cdiv(keys, count_here.shape[1]), axis=1)[:, :keys]
    own_heads(normed, w, count, q, k, v, top, total, acc, att)


def block_time(index, core, queries, rows):
    edge = jnp.where(core == 0, -EXT, rows)
    return jnp.where(index < queries, index + core * (rows - queries), index - queries + edge)


def block_mask(index, core, queries, rows, count):
    tm, last = lax.axis_index("tm"), lax.axis_size("tm") - 1
    time = block_time(index, core, queries, rows)
    low = jnp.where(tm > 0, -EXT, 0)
    high = jnp.where(tm < last, rows + EXT, count)
    return jnp.where((time >= low) & (time < high), 1.0, 0.0)


def warm_kernel(own_shift, other_shift):
    p = lax.axis_index("mp")
    for out, core in ((own_shift, p), (other_shift, 1 - p)):
        half, width = out.shape[0] // len(MOVED), out.shape[1]
        time = block_time(positions((1, width), 1, 0), core, width - EXT, 2 * half)
        for i, tap in enumerate(MOVED):
            row = positions((half, width), 0, core * half + tap - KERNEL // 2)
            out[i * half : (i + 1) * half, :] = jnp.where(row == time, 1.0, 0.0).astype(BF16)


def mask_shift(shift, core, count, out, mask_out):
    half, width = out.shape[0] // len(MOVED), out.shape[1]
    queries, rows = width - EXT, 2 * half
    mask = block_mask(positions((1, width), 1, 0), core, queries, rows, count[0:1, :width])
    mask = mask.astype(BF16)
    for i in range(len(MOVED)):
        at = slice(i * half, (i + 1) * half)
        out[at, :] = shift[at, :] * mask
    index = positions(mask_out.shape, 0, 0)
    mask_out[...] = block_mask(index, core, queries, rows, count[0:1, : mask_out.shape[1]])


def second_kernel(
    normed,
    w,
    count_here,
    own_base,
    other_base,
    q,
    k,
    v,
    top,
    total,
    acc,
    att,
    own_shift,
    other_shift,
    own_mask,
    other_mask,
):
    p = lax.axis_index("mp")
    first_kernel(normed, w, count_here, q, k, v, top, total, acc, att)
    mask_shift(own_base, p, count_here, own_shift, own_mask)
    mask_shift(other_base, 1 - p, count_here, other_shift, other_mask)


def halo_kernel(halo, frames, gain, bias, wo, *refs):
    parts = (refs[:8], refs[8:16])
    send, att_all, normed, kx, vx = refs[16:]
    p = lax.axis_index("mp")
    last = lax.axis_size("tm") - 1
    tm = lax.axis_index("tm")
    rows, queries, keys = frames.shape[0], refs[1].shape[0], refs[2].shape[0]
    width = refs[1].shape[1]
    heads = width // HEAD_DIM
    present = jnp.where(p == 0, tm > 0, tm < last)
    norms = (gain[...], bias[...])
    blocks = range(frames.shape[1] // LANES)
    ext = halo_rows(halo, (CTX - EXT) * (1 - p), EXT, blocks)
    row = positions(ext.shape, 0, 0)
    fixed = jnp.where(row == 0, gain[...], jnp.where(row == 1, bias[...], 0.0))
    left = jnp.concatenate([ext * gain[...], fixed], axis=0)
    high = left.astype(BF16)
    left = left - high.astype(F32)
    middle = left.astype(BF16)
    low = (left - middle.astype(F32)).astype(BF16)
    left = jnp.concatenate([high, middle, low], axis=0)
    ext_mean = jnp.mean(ext, axis=-1, keepdims=True)
    ext_center = ext - ext_mean
    ext_scale = lax.rsqrt(jnp.mean(ext_center * ext_center, axis=-1, keepdims=True) + 1e-05)
    q_ext = []
    for w, *_ in parts:
        thirds = dot(left, w[0])
        whole = thirds[: 2 * EXT] + thirds[2 * EXT : 4 * EXT] + thirds[4 * EXT :]
        q = (whole[:EXT] - ext_mean * whole[EXT : EXT + 1]) * ext_scale
        q_ext.append((q + whole[EXT + 1 : EXT + 2]) * SCALE)
    q_ext = jnp.concatenate(q_ext, axis=1)
    near = halo_rows(halo, 0, CTX, blocks)
    normed[:CTX, :] = layer_normed(near, *norms).astype(BF16)
    far = halo[len(blocks) * CTX :, :].astype(F32)
    far = jnp.concatenate([far[i * FAR : (i + 1) * FAR] for i in blocks], axis=1)
    far = jnp.concatenate([far, jnp.zeros((EXT - FAR, far.shape[1]), F32)], axis=0)
    normed[CTX:, :] = layer_normed(far, *norms).astype(BF16)
    near_at = jnp.where(p == 0, -CTX, rows)
    far_at = jnp.where(p == 0, -(CTX + FAR), rows + CTX)
    ext_at = jnp.where(p == 0, -EXT, rows)
    part = rows_at(p * (queries - CTX), CTX)
    rest = rows_at((1 - p) * CTX, queries - CTX)
    own = rows_at(p * (keys - CTX), CTX)
    own_pos = p * (rows - CTX)
    blank = jnp.zeros((PAD - EXT, width), F32)
    query_pos = positions((CTX, CTX), 0, p * (rows - CTX))
    near_pos = positions((CTX, CTX), 1, near_at)
    allowed = (jnp.abs(near_pos - query_pos) <= CTX) & present
    each = [
        (side, head, slice(head * HEAD_DIM, (head + 1) * HEAD_DIM))
        for side in range(2)
        for head in range(heads)
    ]

    def lanes_of(side, at):
        return slice(side * width + at.start, side * width + at.stop)

    for side, (w, q, k, v, top_own, total_own, acc_own, att) in enumerate(parts):
        to = slice(side * width, (side + 1) * width)
        kx[CTX + PAD :, to] = k[own, :]
        vx[CTX + PAD :, to] = v[own, :]
        att_all[CTX + PAD : CTX + PAD + queries - CTX, to] = att[rest, :]

    def project(x, i, sides):
        for side in sides:
            w = parts[side][0]
            to = slice(side * width, (side + 1) * width)
            got = dot(normed[...], w[i])
            x[:CTX, to] = got[:CTX].astype(BF16)
            x[CTX : CTX + PAD, to] = jnp.concatenate([got[CTX:], blank], axis=0).astype(BF16)

    scores = []
    project(kx, 1, (0, 1))
    deep = 2 * heads * EXT
    tiled = jnp.concatenate([q_ext] * (2 * heads), axis=0)
    head_of_row = positions(tiled.shape, 0, 0) // EXT
    head_of_lane = positions(tiled.shape, 1, 0) // HEAD_DIM
    tiled = jnp.where(head_of_row == head_of_lane, tiled, 0.0).astype(BF16)
    project(vx, 2, (0,))
    scores += [
        dot_t(parts[i][1][part, at], kx[:CTX, lanes_of(i, at)]) for i, head, at in each if i == 0
    ]
    scores += [
        dot_t(parts[i][1][part, at], kx[:CTX, lanes_of(i, at)]) for i, head, at in each if i == 1
    ]
    ext_scores = dot_t(tiled, kx[...])
    project(vx, 2, (1,))
    raised, total, faded = [], [], []
    for (side, head, at), score in zip(each, scores):
        top_own, total_own = parts[side][4], parts[side][5]
        score = jnp.where(allowed, score, NEG)
        before = top_own[head, part, :]
        top = jnp.maximum(before, jnp.max(score, axis=-1, keepdims=True))
        up = jnp.exp2(score - top)
        faded.append(jnp.exp2(before - top))
        total.append(
            total_own[head, part, :] * faded[-1] + jnp.sum(up, axis=-1, keepdims=True)
        )
        raised.append(up.astype(BF16))
    column = positions((deep, SPAN), 1, 0)
    key_pos = jnp.where(
        column < CTX,
        column + near_at,
        jnp.where(column < CTX + FAR, column - CTX + far_at, column - (CTX + PAD) + own_pos),
    )
    row_pos = positions((deep, SPAN), 0, 0) % EXT + ext_at
    seen = (jnp.abs(key_pos - row_pos) <= CTX) & ((column < CTX + FAR) | (column >= CTX + PAD))
    ext_scores = jnp.where(seen, ext_scores, NEG)
    ext_up = jnp.exp2(ext_scores - jnp.max(ext_scores, axis=-1, keepdims=True))
    ext_total = jnp.sum(ext_up, axis=-1, keepdims=True)
    gathered = [
        dot(up, vx[:CTX, lanes_of(side, at)]) for (side, head, at), up in zip(each, raised)
    ]
    spread = dot(ext_up.astype(BF16), vx[...]) * (1.0 / ext_total)
    for i, (side, head, at) in enumerate(each):
        acc = parts[side][6][part, at] * faded[i] + gathered[i]
        att_all[:CTX, lanes_of(side, at)] = (acc / total[i]).astype(BF16)
    ext_att = jnp.concatenate(
        [
            spread[h * EXT : (h + 1) * EXT, h * HEAD_DIM : (h + 1) * HEAD_DIM]
            for h in range(2 * heads)
        ],
        axis=1,
    )
    att_all[CTX : CTX + PAD, :] = jnp.concatenate(
        [ext_att, jnp.zeros_like(ext_att)], axis=0
    ).astype(BF16)
    mix(att_all, frames, halo, wo, 1 - p, send)


def mix(att_all, frames, halo, wo, columns, out):
    p = lax.axis_index("mp")
    rows, width = frames.shape[0], out.shape[1]
    queries = out.shape[0] - EXT
    other = queries - CTX
    lanes = pl.ds(pl.multiple_of(columns * width, width), width)
    projected = 0.0
    for side in range(2):
        for at in range(0, width, 2 * HEAD_DIM):
            first = (p if side == 0 else 1 - p) * width + at
            pair = wo[pl.ds(pl.multiple_of(first, 128), 2 * HEAD_DIM), :]
            at += side * width
            projected = projected + dot(att_all[:, at : at + 2 * HEAD_DIM], pair)

    def put(plain, to, size, at):
        out[rows_at(to, size), :] = (plain + projected[at : at + size]).astype(BF16)

    def own(at, size):
        return frames[rows_at(p * (rows - queries) + at, size), lanes].astype(F32)

    put(own(p * other, CTX), p * other, CTX, 0)
    count = width // LANES
    blocks = [columns * count + i for i in range(count)]
    put(halo_rows(halo, (CTX - EXT) * (1 - p), EXT, blocks), queries, EXT, CTX)
    put(own((1 - p) * CTX, other), (1 - p) * CTX, other, CTX + PAD)


def keep_kernel(att_all, frames, halo, wo, keep):
    mix(att_all, frames, halo, wo, lax.axis_index("mp"), keep)


def convolved(block, core, shift_by, mask, weight, scale, shift, store):
    half = shift_by.shape[0] // len(MOVED)
    rows = rows_at(core * (block.shape[0] - EXT - half), half)
    step = 2 * LANES
    valid = jnp.concatenate([mask[rows, :]] * (step // mask.shape[1]), axis=1)
    for at in range(0, block.shape[1], step):
        lanes = slice(at, at + step)
        gain = 0.5 * scale[:, lanes]
        plain = block[rows, lanes].astype(F32)
        u = plain * valid * (weight[MIDDLE : MIDDLE + 1, lanes] * gain) + 0.5 * shift[:, lanes]
        for first in range(0, len(MOVED), GROUP):
            group = MOVED[first : first + GROUP]
            moved = dot(shift_by[first * half : (first + len(group)) * half, :], block[:, lanes])
            for i, tap in enumerate(group):
                part = moved[i * half : (i + 1) * half]
                u = u + part * (weight[tap : tap + 1, lanes] * gain)
        store(lanes, (plain + (u + u * jnp.tanh(u))).astype(BF16))


def own_conv_kernel(keep, shift_by, mask, weight, scale, shift, out):
    def store(lanes, value):
        out[:, lanes] = value

    core = lax.axis_index("mp")
    convolved(keep, core, shift_by, mask, weight, scale, shift, store)


def other_conv_kernel(got, done, shift_by, mask, weight, scale, shift, out, block, sems):
    core = 1 - lax.axis_index("mp")
    half = done.shape[0]
    first = pltpu.make_async_copy(done, out.at[rows_at((1 - core) * half, half), :], sems.at[0])
    first.start()
    copies = [first]

    def store(lanes, value):
        block[:, lanes] = value
        copies.append(
            pltpu.make_async_copy(
                block.at[:, lanes], out.at[rows_at(core * half, half), lanes], sems.at[len(copies)]
            )
        )
        copies[-1].start()

    convolved(got, core, shift_by, mask, weight, scale, shift, store)
    for copy in copies:
        copy.wait()


def call(kernel, out_shape, in_specs, out_specs, scratch=(), flops=0, size=0, exps=0, limit=16):
    return pl.pallas_call(
        kernel,
        out_shape=out_shape,
        in_specs=in_specs,
        out_specs=out_specs,
        scratch_shapes=scratch,
        compiler_params=pltpu.CompilerParams(vmem_limit_bytes=limit << 20),
        cost_estimate=pl.CostEstimate(flops=flops, bytes_accessed=size, transcendentals=exps),
    )


def compute(frames, valid, norm_gain, norm_bias, w_qkv, w_out, conv_weight, conv_scale, conv_shift):
    rows, model = frames.shape
    width = w_qkv.shape[2]
    heads = width // HEAD_DIM
    count = lax.axis_size("tm")
    half = rows // 2
    queries = half + EXT
    keys = half + EXT + CTX
    block = queries + EXT
    assert rows >= HALO + CTX and rows % 32 == 0
    shaped = jax.ShapeDtypeStruct
    pairs = [(1, 0), (2 * count - 2, 2 * count - 1)]
    for i in range(count - 1):
        pairs += [(2 * i, 2 * (i + 1)), (2 * (i + 1) + 1, 2 * i + 1)]
    other = [(0, 1), (1, 0)]
    shift_shapes = (shaped((len(MOVED) * half, block), BF16),) * 2
    shifts = call(warm_kernel, shift_shapes, [], (VMEM,) * 2, flops=WARM_FLOPS)()
    sent = call(
        pick_kernel,
        shaped(((CTX + FAR) * (model // LANES), LANES), BF16),
        [VMEM, ANY],
        VMEM,
        flops=PICK_FLOPS,
    )(frames, shifts[0])
    halo = lax.ppermute(sent, ("tm", "mp"), pairs)
    w_other = lax.ppermute(w_qkv, "mp", other)
    wo_other = lax.ppermute(w_out, "mp", other)
    gain, bias = norm_gain.reshape(1, model), norm_bias.reshape(1, model)
    results = (
        shaped((queries, width), BF16),
        shaped((keys, width), BF16),
        shaped((keys, width), BF16),
        shaped((heads, queries, HEAD_DIM), F32),
        shaped((heads, queries, HEAD_DIM), F32),
        shaped((queries, width), F32),
        shaped((queries, width), BF16),
    )
    normed, count_here = call(
        norm_kernel,
        (shaped((keys, model), BF16), shaped((8, 256), jnp.int32)),
        [VMEM, SMEM, VMEM, VMEM],
        (VMEM,) * 2,
        flops=NORM_FLOPS,
        size=1_000_000,
    )(frames, valid, gain, bias)
    mine = call(
        first_kernel,
        results,
        [VMEM] * 3,
        (VMEM,) * 7,
        flops=1_300_000_000,
        size=4_000_000,
        exps=300_000,
    )(normed, w_qkv, count_here)
    second = call(
        second_kernel,
        results + shift_shapes + (shaped((block, LANES), F32),) * 2,
        [VMEM] * 5,
        (VMEM,) * 11,
        flops=1_300_000_000,
        size=4_000_000,
        exps=300_000,
    )(normed, w_other, count_here, *shifts)
    theirs, (own_shift, other_shift, own_mask, other_mask) = second[:7], second[7:]
    send, att_all = call(
        halo_kernel,
        (shaped((block, width), BF16), shaped((pl.cdiv(queries, 16) * 16 + PAD, model), BF16)),
        [VMEM] * 21,
        (VMEM,) * 2,
        [
            pltpu.VMEM((HALO, model), BF16),
            pltpu.VMEM((SPAN, model), BF16),
            pltpu.VMEM((SPAN, model), BF16),
        ],
        flops=1_500_000_000,
        size=10_000_000,
        exps=300_000,
    )(halo, frames, gain, bias, wo_other, w_qkv, *mine, w_other, *theirs)
    got = lax.ppermute(send, "mp", other)
    keep = call(
        keep_kernel,
        shaped((block, width), BF16),
        [VMEM] * 4,
        VMEM,
        flops=200_000_000,
        size=1_000_000,
    )(att_all, frames, halo, w_out)
    weights = (conv_weight, conv_scale.reshape(1, width), conv_shift.reshape(1, width))
    done = call(
        own_conv_kernel,
        shaped((half, width), BF16),
        [VMEM] * 6,
        VMEM,
        flops=270_000_000,
        size=1_000_000,
    )(keep, own_shift, own_mask, *weights)
    return call(
        other_conv_kernel,
        shaped((rows, width), BF16),
        [VMEM] * 7,
        ANY,
        [pltpu.VMEM((half, width), BF16), pltpu.SemaphoreType.DMA((1 + width // 256,))],
        flops=270_000_000,
        size=1_000_000,
    )(got, done, other_shift, other_mask, *weights)


def solution(mesh):
    placed = (
        P("tm", None),
        P("tm"),
        P(),
        P(),
        P(None, None, "mp"),
        P(None, "mp"),
        P(None, "mp"),
        P("mp"),
        P("mp"),
    )
    return jax.shard_map(
        compute, mesh=mesh, in_specs=placed, out_specs=P("tm", "mp"), check_vma=False
    )
```

```python
import math

import jax
import jax.numpy as jnp
from jax import lax
from jax.experimental import pallas as pl
from jax.experimental.pallas import tpu as pltpu
from jax.sharding import PartitionSpec as P

HEAD_DIM = 128
CTX = 128
KERNEL = 9
EXT = 8
HALO = CTX + EXT
FAR = KERNEL // 2
LANES = 128
MIDDLE = KERNEL // 2
MOVED = [tap for tap in range(KERNEL) if tap != MIDDLE]
PAD = 16
SPAN = CTX + PAD + CTX
NEG = -1e30
GROUP = 2
WARM_FLOPS, PICK_FLOPS, NORM_FLOPS = 1_500_000_000, 1_000_000_000, 1_500_000_000
SCALE = math.log2(math.e) / math.sqrt(HEAD_DIM)
VMEM = pl.BlockSpec(memory_space=pltpu.VMEM)
ANY = pl.BlockSpec(memory_space=pl.ANY)
SMEM = pl.BlockSpec(memory_space=pltpu.SMEM)
F32, BF16 = jnp.float32, jnp.bfloat16


def layer_normed(values, gain, bias):
    center = values - jnp.mean(values, axis=-1, keepdims=True)
    spread = jnp.mean(center * center, axis=-1, keepdims=True)
    return center * lax.rsqrt(spread + 1e-05) * gain + bias


def norm_rows(source, source_at, target, target_at, count, gain, bias):
    step = 16
    for at in range(0, count, step):
        size = min(step, count - at)
        values = source[rows_at(source_at + at, size), :].astype(F32)
        target[target_at + at : target_at + at + size, :] = layer_normed(
            values, gain, bias
        ).astype(BF16)


def dot(a, b):
    return jnp.dot(a, b, preferred_element_type=F32)


def dot_t(a, b):
    return lax.dot_general(a, b, (((1,), (1,)), ((), ())), preferred_element_type=F32)


def positions(shape, dim, start):
    return lax.broadcasted_iota(jnp.int32, shape, dim) + start


def rows_at(start, size):
    return pl.ds(pl.multiple_of(start, 8), size)


def lane_blocks(width):
    return [slice(at, at + LANES) for at in range(0, width, LANES)]


def pick_kernel(frames, after, sent):
    p = lax.axis_index("mp")
    rows, width = frames.shape
    blocks = lane_blocks(width)
    near = rows_at((1 - p) * (rows - CTX), CTX)
    for i, lanes in enumerate(blocks):
        sent[i * CTX : (i + 1) * CTX, :] = frames[near, lanes]
    far = frames[rows_at((1 - p) * (rows - HALO) + p * CTX, EXT), :].astype(F32)
    far = jnp.where(p == 0, pltpu.roll(far, EXT - FAR, 0), far)
    sent[len(blocks) * CTX :, :] = jnp.concatenate(
        [far[:FAR, lanes] for lanes in blocks], axis=0
    ).astype(BF16)


def halo_rows(halo, start, size, blocks):
    return jnp.concatenate(
        [halo[rows_at(i * CTX + start, size), :].astype(F32) for i in blocks], axis=1
    )


def own_heads(normed, w, count, q_out, k_out, v_out, top_out, total_out, acc_out, att_out):
    p = lax.axis_index("mp")
    keys, queries = k_out.shape[0], q_out.shape[0]
    rows = 2 * (queries - EXT)
    key_at, query_at = p * (rows - keys), p * (rows - queries)
    k_out[...] = dot(normed[...], w[1]).astype(BF16)
    picked = normed[pl.ds(pl.multiple_of(p * (keys - queries), 16), queries), :]
    q_out[...] = (dot(picked, w[0]) * SCALE).astype(BF16)
    v_out[...] = dot(normed[...], w[2]).astype(BF16)
    key_pos = positions((queries, keys), 1, key_at)
    query_pos = positions((queries, keys), 0, query_at)
    allowed = (jnp.abs(key_pos - query_pos) <= CTX) & (key_pos < count)
    for head in range(q_out.shape[1] // HEAD_DIM):
        at = slice(head * HEAD_DIM, (head + 1) * HEAD_DIM)
        scores = dot_t(q_out[:, at], k_out[:, at])
        scores = jnp.where(allowed, scores, NEG)
        top = jnp.max(scores, axis=-1, keepdims=True)
        raised = jnp.exp2(scores - top)
        total = jnp.sum(raised, axis=-1, keepdims=True)
        top_out[head] = jnp.broadcast_to(top, (queries, HEAD_DIM))
        total_out[head] = jnp.broadcast_to(total, (queries, HEAD_DIM))
        acc = dot(raised.astype(BF16), v_out[:, at])
        acc_out[:, at] = acc
        att_out[:, at] = (acc * (1.0 / total)).astype(BF16)


def norm_kernel(frames, valid, gain, bias, normed, count_here):
    p = lax.axis_index("mp")
    rows, keys = frames.shape[0], normed.shape[0]
    low, high = jnp.int32(0), jnp.int32(rows)
    for _ in range(rows.bit_length()):
        middle = (low + high) // 2
        one = valid[jnp.minimum(middle, rows - 1)] > 0
        open_ = low < high
        low = jnp.where(open_ & one, middle + 1, low)
        high = jnp.where(open_ & jnp.logical_not(one), middle, high)
    count_here[...] = jnp.full(count_here.shape, low, jnp.int32)
    norm_rows(frames, p * (rows - keys), normed, 0, keys, gain[...], bias[...])


def first_kernel(normed, w, count_here, q, k, v, top, total, acc, att):
    keys = k.shape[0]
    count = jnp.concatenate([count_here[0:1, :]] * pl.cdiv(keys, count_here.shape[1]), axis=1)[:, :keys]
    own_heads(normed, w, count, q, k, v, top, total, acc, att)


def block_time(index, core, queries, rows):
    edge = jnp.where(core == 0, -EXT, rows)
    return jnp.where(index < queries, index + core * (rows - queries), index - queries + edge)


def block_mask(index, core, queries, rows, count):
    tm, last = lax.axis_index("tm"), lax.axis_size("tm") - 1
    time = block_time(index, core, queries, rows)
    low = jnp.where(tm > 0, -EXT, 0)
    high = jnp.where(tm < last, rows + EXT, count)
    return jnp.where((time >= low) & (time < high), 1.0, 0.0)


def warm_kernel(own_shift, other_shift):
    p = lax.axis_index("mp")
    for out, core in ((own_shift, p), (other_shift, 1 - p)):
        half, width = out.shape[0] // len(MOVED), out.shape[1]
        time = block_time(positions((1, width), 1, 0), core, width - EXT, 2 * half)
        for i, tap in enumerate(MOVED):
            row = positions((half, width), 0, core * half + tap - KERNEL // 2)
            out[i * half : (i + 1) * half, :] = jnp.where(row == time, 1.0, 0.0).astype(BF16)


def mask_shift(shift, core, count, out, mask_out):
    half, width = out.shape[0] // len(MOVED), out.shape[1]
    queries, rows = width - EXT, 2 * half
    mask = block_mask(positions((1, width), 1, 0), core, queries, rows, count[0:1, :width])
    mask = mask.astype(BF16)
    for i in range(len(MOVED)):
        at = slice(i * half, (i + 1) * half)
        out[at, :] = shift[at, :] * mask
    index = positions(mask_out.shape, 0, 0)
    mask_out[...] = block_mask(index, core, queries, rows, count[0:1, : mask_out.shape[1]])


def second_kernel(
    normed,
    w,
    count_here,
    own_base,
    other_base,
    q,
    k,
    v,
    top,
    total,
    acc,
    att,
    own_shift,
    other_shift,
    own_mask,
    other_mask,
):
    p = lax.axis_index("mp")
    first_kernel(normed, w, count_here, q, k, v, top, total, acc, att)
    mask_shift(own_base, p, count_here, own_shift, own_mask)
    mask_shift(other_base, 1 - p, count_here, other_shift, other_mask)


def halo_kernel(halo, frames, gain, bias, wo, *refs):
    parts = (refs[:8], refs[8:16])
    send, att_all, normed, kx, vx = refs[16:]
    p = lax.axis_index("mp")
    last = lax.axis_size("tm") - 1
    tm = lax.axis_index("tm")
    rows, queries, keys = frames.shape[0], refs[1].shape[0], refs[2].shape[0]
    width = refs[1].shape[1]
    heads = width // HEAD_DIM
    present = jnp.where(p == 0, tm > 0, tm < last)
    norms = (gain[...], bias[...])
    blocks = range(frames.shape[1] // LANES)
    ext = halo_rows(halo, (CTX - EXT) * (1 - p), EXT, blocks)
    row = positions(ext.shape, 0, 0)
    fixed = jnp.where(row == 0, gain[...], jnp.where(row == 1, bias[...], 0.0))
    left = jnp.concatenate([ext * gain[...], fixed], axis=0)
    high = left.astype(BF16)
    left = left - high.astype(F32)
    middle = left.astype(BF16)
    low = (left - middle.astype(F32)).astype(BF16)
    left = jnp.concatenate([high, middle, low], axis=0)
    ext_mean = jnp.mean(ext, axis=-1, keepdims=True)
    ext_center = ext - ext_mean
    ext_scale = lax.rsqrt(jnp.mean(ext_center * ext_center, axis=-1, keepdims=True) + 1e-05)
    q_ext = []
    for w, *_ in parts:
        thirds = dot(left, w[0])
        whole = thirds[: 2 * EXT] + thirds[2 * EXT : 4 * EXT] + thirds[4 * EXT :]
        q = (whole[:EXT] - ext_mean * whole[EXT : EXT + 1]) * ext_scale
        q_ext.append((q + whole[EXT + 1 : EXT + 2]) * SCALE)
    q_ext = jnp.concatenate(q_ext, axis=1)
    near = halo_rows(halo, 0, CTX, blocks)
    normed[:CTX, :] = layer_normed(near, *norms).astype(BF16)
    far = halo[len(blocks) * CTX :, :].astype(F32)
    far = jnp.concatenate([far[i * FAR : (i + 1) * FAR] for i in blocks], axis=1)
    far = jnp.concatenate([far, jnp.zeros((EXT - FAR, far.shape[1]), F32)], axis=0)
    normed[CTX:, :] = layer_normed(far, *norms).astype(BF16)
    near_at = jnp.where(p == 0, -CTX, rows)
    far_at = jnp.where(p == 0, -(CTX + FAR), rows + CTX)
    ext_at = jnp.where(p == 0, -EXT, rows)
    part = rows_at(p * (queries - CTX), CTX)
    rest = rows_at((1 - p) * CTX, queries - CTX)
    own = rows_at(p * (keys - CTX), CTX)
    own_pos = p * (rows - CTX)
    blank = jnp.zeros((PAD - EXT, width), F32)
    query_pos = positions((CTX, CTX), 0, p * (rows - CTX))
    near_pos = positions((CTX, CTX), 1, near_at)
    allowed = (jnp.abs(near_pos - query_pos) <= CTX) & present
    each = [
        (side, head, slice(head * HEAD_DIM, (head + 1) * HEAD_DIM))
        for side in range(2)
        for head in range(heads)
    ]

    def lanes_of(side, at):
        return slice(side * width + at.start, side * width + at.stop)

    for side, (w, q, k, v, top_own, total_own, acc_own, att) in enumerate(parts):
        to = slice(side * width, (side + 1) * width)
        kx[CTX + PAD :, to] = k[own, :]
        vx[CTX + PAD :, to] = v[own, :]
        att_all[CTX + PAD : CTX + PAD + queries - CTX, to] = att[rest, :]

    def project(x, i, sides):
        for side in sides:
            w = parts[side][0]
            to = slice(side * width, (side + 1) * width)
            got = dot(normed[...], w[i])
            x[:CTX, to] = got[:CTX].astype(BF16)
            x[CTX : CTX + PAD, to] = jnp.concatenate([got[CTX:], blank], axis=0).astype(BF16)

    scores = []
    project(kx, 1, (0, 1))
    deep = 2 * heads * EXT
    tiled = jnp.concatenate([q_ext] * (2 * heads), axis=0)
    head_of_row = positions(tiled.shape, 0, 0) // EXT
    head_of_lane = positions(tiled.shape, 1, 0) // HEAD_DIM
    tiled = jnp.where(head_of_row == head_of_lane, tiled, 0.0).astype(BF16)
    project(vx, 2, (0,))
    scores += [
        dot_t(parts[i][1][part, at], kx[:CTX, lanes_of(i, at)]) for i, head, at in each if i == 0
    ]
    scores += [
        dot_t(parts[i][1][part, at], kx[:CTX, lanes_of(i, at)]) for i, head, at in each if i == 1
    ]
    ext_scores = dot_t(tiled, kx[...])
    project(vx, 2, (1,))
    raised, total, faded = [], [], []
    for (side, head, at), score in zip(each, scores):
        top_own, total_own = parts[side][4], parts[side][5]
        score = jnp.where(allowed, score, NEG)
        before = top_own[head, part, :]
        top = jnp.maximum(before, jnp.max(score, axis=-1, keepdims=True))
        up = jnp.exp2(score - top)
        faded.append(jnp.exp2(before - top))
        total.append(
            total_own[head, part, :] * faded[-1] + jnp.sum(up, axis=-1, keepdims=True)
        )
        raised.append(up.astype(BF16))
    column = positions((deep, SPAN), 1, 0)
    key_pos = jnp.where(
        column < CTX,
        column + near_at,
        jnp.where(column < CTX + FAR, column - CTX + far_at, column - (CTX + PAD) + own_pos),
    )
    row_pos = positions((deep, SPAN), 0, 0) % EXT + ext_at
    seen = (jnp.abs(key_pos - row_pos) <= CTX) & ((column < CTX + FAR) | (column >= CTX + PAD))
    ext_scores = jnp.where(seen, ext_scores, NEG)
    ext_up = jnp.exp2(ext_scores - jnp.max(ext_scores, axis=-1, keepdims=True))
    ext_total = jnp.sum(ext_up, axis=-1, keepdims=True)
    gathered = [
        dot(up, vx[:CTX, lanes_of(side, at)]) for (side, head, at), up in zip(each, raised)
    ]
    spread = dot(ext_up.astype(BF16), vx[...]) * (1.0 / ext_total)
    for i, (side, head, at) in enumerate(each):
        acc = parts[side][6][part, at] * faded[i] + gathered[i]
        att_all[:CTX, lanes_of(side, at)] = (acc / total[i]).astype(BF16)
    ext_att = jnp.concatenate(
        [
            spread[h * EXT : (h + 1) * EXT, h * HEAD_DIM : (h + 1) * HEAD_DIM]
            for h in range(2 * heads)
        ],
        axis=1,
    )
    att_all[CTX : CTX + PAD, :] = jnp.concatenate(
        [ext_att, jnp.zeros_like(ext_att)], axis=0
    ).astype(BF16)
    mix(att_all, frames, halo, wo, 1 - p, send)


def mix(att_all, frames, halo, wo, columns, out):
    p = lax.axis_index("mp")
    rows, width = frames.shape[0], out.shape[1]
    queries = out.shape[0] - EXT
    other = queries - CTX
    lanes = pl.ds(pl.multiple_of(columns * width, width), width)
    projected = 0.0
    for side in range(2):
        for at in range(0, width, 2 * HEAD_DIM):
            first = (p if side == 0 else 1 - p) * width + at
            pair = wo[pl.ds(pl.multiple_of(first, 128), 2 * HEAD_DIM), :]
            at += side * width
            projected = projected + dot(att_all[:, at : at + 2 * HEAD_DIM], pair)

    def put(plain, to, size, at):
        out[rows_at(to, size), :] = (plain + projected[at : at + size]).astype(BF16)

    def own(at, size):
        return frames[rows_at(p * (rows - queries) + at, size), lanes].astype(F32)

    put(own(p * other, CTX), p * other, CTX, 0)
    count = width // LANES
    blocks = [columns * count + i for i in range(count)]
    put(halo_rows(halo, (CTX - EXT) * (1 - p), EXT, blocks), queries, EXT, CTX)
    put(own((1 - p) * CTX, other), (1 - p) * CTX, other, CTX + PAD)


def keep_kernel(att_all, frames, halo, wo, keep):
    mix(att_all, frames, halo, wo, lax.axis_index("mp"), keep)


def convolved(block, core, shift_by, mask, weight, scale, shift, store):
    half = shift_by.shape[0] // len(MOVED)
    rows = rows_at(core * (block.shape[0] - EXT - half), half)
    step = 2 * LANES
    valid = jnp.concatenate([mask[rows, :]] * (step // mask.shape[1]), axis=1)
    for at in range(0, block.shape[1], step):
        lanes = slice(at, at + step)
        gain = 0.5 * scale[:, lanes]
        plain = block[rows, lanes].astype(F32)
        u = plain * valid * (weight[MIDDLE : MIDDLE + 1, lanes] * gain) + 0.5 * shift[:, lanes]
        for first in range(0, len(MOVED), GROUP):
            group = MOVED[first : first + GROUP]
            moved = dot(shift_by[first * half : (first + len(group)) * half, :], block[:, lanes])
            for i, tap in enumerate(group):
                part = moved[i * half : (i + 1) * half]
                u = u + part * (weight[tap : tap + 1, lanes] * gain)
        store(lanes, (plain + (u + u * jnp.tanh(u))).astype(BF16))


def own_conv_kernel(keep, shift_by, mask, weight, scale, shift, out):
    def store(lanes, value):
        out[:, lanes] = value

    core = lax.axis_index("mp")
    convolved(keep, core, shift_by, mask, weight, scale, shift, store)


def other_conv_kernel(got, done, shift_by, mask, weight, scale, shift, out):
    core = 1 - lax.axis_index("mp")
    half = done.shape[0]
    out[rows_at((1 - core) * half, half), :] = done[...]

    def store(lanes, value):
        out[rows_at(core * half, half), lanes] = value

    convolved(got, core, shift_by, mask, weight, scale, shift, store)


def call(kernel, out_shape, in_specs, out_specs, scratch=(), flops=0, size=0, exps=0, limit=16):
    return pl.pallas_call(
        kernel,
        out_shape=out_shape,
        in_specs=in_specs,
        out_specs=out_specs,
        scratch_shapes=scratch,
        compiler_params=pltpu.CompilerParams(vmem_limit_bytes=limit << 20),
        cost_estimate=pl.CostEstimate(flops=flops, bytes_accessed=size, transcendentals=exps),
    )


def compute(frames, valid, norm_gain, norm_bias, w_qkv, w_out, conv_weight, conv_scale, conv_shift):
    rows, model = frames.shape
    width = w_qkv.shape[2]
    heads = width // HEAD_DIM
    count = lax.axis_size("tm")
    half = rows // 2
    queries = half + EXT
    keys = half + EXT + CTX
    block = queries + EXT
    assert rows >= HALO + CTX and rows % 32 == 0
    shaped = jax.ShapeDtypeStruct
    pairs = [(1, 0), (2 * count - 2, 2 * count - 1)]
    for i in range(count - 1):
        pairs += [(2 * i, 2 * (i + 1)), (2 * (i + 1) + 1, 2 * i + 1)]
    other = [(0, 1), (1, 0)]
    shift_shapes = (shaped((len(MOVED) * half, block), BF16),) * 2
    shifts = call(warm_kernel, shift_shapes, [], (VMEM,) * 2, flops=WARM_FLOPS)()
    sent = call(
        pick_kernel,
        shaped(((CTX + FAR) * (model // LANES), LANES), BF16),
        [VMEM, ANY],
        VMEM,
        flops=PICK_FLOPS,
    )(frames, shifts[0])
    halo = lax.ppermute(sent, ("tm", "mp"), pairs)
    w_other = lax.ppermute(w_qkv, "mp", other)
    wo_other = lax.ppermute(w_out, "mp", other)
    gain, bias = norm_gain.reshape(1, model), norm_bias.reshape(1, model)
    results = (
        shaped((queries, width), BF16),
        shaped((keys, width), BF16),
        shaped((keys, width), BF16),
        shaped((heads, queries, HEAD_DIM), F32),
        shaped((heads, queries, HEAD_DIM), F32),
        shaped((queries, width), F32),
        shaped((queries, width), BF16),
    )
    normed, count_here = call(
        norm_kernel,
        (shaped((keys, model), BF16), shaped((8, 256), jnp.int32)),
        [VMEM, SMEM, VMEM, VMEM],
        (VMEM,) * 2,
        flops=NORM_FLOPS,
        size=1_000_000,
    )(frames, valid, gain, bias)
    mine = call(
        first_kernel,
        results,
        [VMEM] * 3,
        (VMEM,) * 7,
        flops=1_300_000_000,
        size=4_000_000,
        exps=300_000,
    )(normed, w_qkv, count_here)
    second = call(
        second_kernel,
        results + shift_shapes + (shaped((block, LANES), F32),) * 2,
        [VMEM] * 5,
        (VMEM,) * 11,
        flops=1_300_000_000,
        size=4_000_000,
        exps=300_000,
    )(normed, w_other, count_here, *shifts)
    theirs, (own_shift, other_shift, own_mask, other_mask) = second[:7], second[7:]
    send, att_all = call(
        halo_kernel,
        (shaped((block, width), BF16), shaped((pl.cdiv(queries, 16) * 16 + PAD, model), BF16)),
        [VMEM] * 21,
        (VMEM,) * 2,
        [
            pltpu.VMEM((HALO, model), BF16),
            pltpu.VMEM((SPAN, model), BF16),
            pltpu.VMEM((SPAN, model), BF16),
        ],
        flops=1_500_000_000,
        size=10_000_000,
        exps=300_000,
    )(halo, frames, gain, bias, wo_other, w_qkv, *mine, w_other, *theirs)
    got = lax.ppermute(send, "mp", other)
    keep = call(
        keep_kernel,
        shaped((block, width), BF16),
        [VMEM] * 4,
        VMEM,
        flops=200_000_000,
        size=1_000_000,
    )(att_all, frames, halo, w_out)
    weights = (conv_weight, conv_scale.reshape(1, width), conv_shift.reshape(1, width))
    done = call(
        own_conv_kernel,
        shaped((half, width), BF16),
        [VMEM] * 6,
        VMEM,
        flops=270_000_000,
        size=1_000_000,
    )(keep, own_shift, own_mask, *weights)
    return call(
        other_conv_kernel,
        shaped((rows, width), BF16),
        [VMEM] * 7,
        VMEM,
        flops=270_000_000,
        size=1_000_000,
    )(got, done, other_shift, other_mask, *weights)


def solution(mesh):
    placed = (
        P("tm", None),
        P("tm"),
        P(),
        P(),
        P(None, None, "mp"),
        P(None, "mp"),
        P(None, "mp"),
        P("mp"),
        P("mp"),
    )
    return jax.shard_map(
        compute, mesh=mesh, in_specs=placed, out_specs=P("tm", "mp"), check_vma=False
    )
```

```python
import math

import jax
import jax.numpy as jnp
from jax import lax
from jax.experimental import pallas as pl
from jax.experimental.pallas import tpu as pltpu
from jax.sharding import PartitionSpec as P

HEAD_DIM = 128
CTX = 128
KERNEL = 9
EXT = 8
HALO = CTX + EXT
FAR = KERNEL // 2
LANES = 128
MIDDLE = KERNEL // 2
MOVED = [tap for tap in range(KERNEL) if tap != MIDDLE]
PAD = 16
SPAN = CTX + PAD + CTX
NEG = -1e30
GROUP = 2
WARM_FLOPS, PICK_FLOPS, NORM_FLOPS = 1_500_000_000, 1_000_000_000, 1_500_000_000
SCALE = math.log2(math.e) / math.sqrt(HEAD_DIM)
VMEM = pl.BlockSpec(memory_space=pltpu.VMEM)
ANY = pl.BlockSpec(memory_space=pl.ANY)
SMEM = pl.BlockSpec(memory_space=pltpu.SMEM)
F32, BF16 = jnp.float32, jnp.bfloat16


def layer_normed(values, gain, bias):
    center = values - jnp.mean(values, axis=-1, keepdims=True)
    spread = jnp.mean(center * center, axis=-1, keepdims=True)
    return center * lax.rsqrt(spread + 1e-05) * gain + bias


def norm_rows(source, source_at, target, target_at, count, gain, bias):
    step = 16
    for at in range(0, count, step):
        size = min(step, count - at)
        values = source[rows_at(source_at + at, size), :].astype(F32)
        target[target_at + at : target_at + at + size, :] = layer_normed(
            values, gain, bias
        ).astype(BF16)


def dot(a, b):
    return jnp.dot(a, b, preferred_element_type=F32)


def dot_t(a, b):
    return lax.dot_general(a, b, (((1,), (1,)), ((), ())), preferred_element_type=F32)


def positions(shape, dim, start):
    return lax.broadcasted_iota(jnp.int32, shape, dim) + start


def rows_at(start, size):
    return pl.ds(pl.multiple_of(start, 8), size)


def lane_blocks(width):
    return [slice(at, at + LANES) for at in range(0, width, LANES)]


def pick_kernel(frames, after, sent):
    p = lax.axis_index("mp")
    rows, width = frames.shape
    blocks = lane_blocks(width)
    near = rows_at((1 - p) * (rows - CTX), CTX)
    for i, lanes in enumerate(blocks):
        sent[i * CTX : (i + 1) * CTX, :] = frames[near, lanes]
    far = frames[rows_at((1 - p) * (rows - HALO) + p * CTX, EXT), :].astype(F32)
    far = jnp.where(p == 0, pltpu.roll(far, EXT - FAR, 0), far)
    sent[len(blocks) * CTX :, :] = jnp.concatenate(
        [far[:FAR, lanes] for lanes in blocks], axis=0
    ).astype(BF16)


def halo_rows(halo, start, size, blocks):
    return jnp.concatenate(
        [halo[rows_at(i * CTX + start, size), :].astype(F32) for i in blocks], axis=1
    )


def own_heads(normed, w, count, q_out, k_out, v_out, top_out, total_out, acc_out, att_out):
    p = lax.axis_index("mp")
    keys, queries = k_out.shape[0], q_out.shape[0]
    rows = 2 * (queries - EXT)
    key_at, query_at = p * (rows - keys), p * (rows - queries)
    k_out[...] = dot(normed[...], w[1]).astype(BF16)
    picked = normed[pl.ds(pl.multiple_of(p * (keys - queries), 16), queries), :]
    q_out[...] = (dot(picked, w[0]) * SCALE).astype(BF16)
    v_out[...] = dot(normed[...], w[2]).astype(BF16)
    key_pos = positions((queries, keys), 1, key_at)
    query_pos = positions((queries, keys), 0, query_at)
    allowed = (jnp.abs(key_pos - query_pos) <= CTX) & (key_pos < count)
    heads = [slice(at, at + HEAD_DIM) for at in range(0, q_out.shape[1], HEAD_DIM)]
    scores = [dot_t(q_out[:, at], k_out[:, at]) for at in heads]
    raised, totals = [], []
    for head, score in enumerate(scores):
        score = jnp.where(allowed, score, NEG)
        top = jnp.max(score, axis=-1, keepdims=True)
        up = jnp.exp2(score - top)
        total = jnp.sum(up, axis=-1, keepdims=True)
        top_out[head] = jnp.broadcast_to(top, (queries, HEAD_DIM))
        total_out[head] = jnp.broadcast_to(total, (queries, HEAD_DIM))
        raised.append(up.astype(BF16))
        totals.append(total)
    for head, at in enumerate(heads):
        acc = dot(raised[head], v_out[:, at])
        acc_out[:, at] = acc
        att_out[:, at] = (acc * (1.0 / totals[head])).astype(BF16)


def norm_kernel(frames, valid, gain, bias, normed, count_here):
    p = lax.axis_index("mp")
    rows, keys = frames.shape[0], normed.shape[0]
    low, high = jnp.int32(0), jnp.int32(rows)
    for _ in range(rows.bit_length()):
        middle = (low + high) // 2
        one = valid[jnp.minimum(middle, rows - 1)] > 0
        open_ = low < high
        low = jnp.where(open_ & one, middle + 1, low)
        high = jnp.where(open_ & jnp.logical_not(one), middle, high)
    count_here[...] = jnp.full(count_here.shape, low, jnp.int32)
    norm_rows(frames, p * (rows - keys), normed, 0, keys, gain[...], bias[...])


def first_kernel(normed, w, count_here, q, k, v, top, total, acc, att):
    keys = k.shape[0]
    count = jnp.concatenate([count_here[0:1, :]] * pl.cdiv(keys, count_here.shape[1]), axis=1)[:, :keys]
    own_heads(normed, w, count, q, k, v, top, total, acc, att)


def block_time(index, core, queries, rows):
    edge = jnp.where(core == 0, -EXT, rows)
    return jnp.where(index < queries, index + core * (rows - queries), index - queries + edge)


def block_mask(index, core, queries, rows, count):
    tm, last = lax.axis_index("tm"), lax.axis_size("tm") - 1
    time = block_time(index, core, queries, rows)
    low = jnp.where(tm > 0, -EXT, 0)
    high = jnp.where(tm < last, rows + EXT, count)
    return jnp.where((time >= low) & (time < high), 1.0, 0.0)


def warm_kernel(own_shift, other_shift):
    p = lax.axis_index("mp")
    for out, core in ((own_shift, p), (other_shift, 1 - p)):
        half, width = out.shape[0] // len(MOVED), out.shape[1]
        time = block_time(positions((1, width), 1, 0), core, width - EXT, 2 * half)
        for i, tap in enumerate(MOVED):
            row = positions((half, width), 0, core * half + tap - KERNEL // 2)
            out[i * half : (i + 1) * half, :] = jnp.where(row == time, 1.0, 0.0).astype(BF16)


def mask_shift(shift, core, count, out, mask_out):
    half, width = out.shape[0] // len(MOVED), out.shape[1]
    queries, rows = width - EXT, 2 * half
    mask = block_mask(positions((1, width), 1, 0), core, queries, rows, count[0:1, :width])
    mask = mask.astype(BF16)
    for i in range(len(MOVED)):
        at = slice(i * half, (i + 1) * half)
        out[at, :] = shift[at, :] * mask
    index = positions(mask_out.shape, 0, 0)
    mask_out[...] = block_mask(index, core, queries, rows, count[0:1, : mask_out.shape[1]])


def second_kernel(
    normed,
    w,
    count_here,
    own_base,
    other_base,
    q,
    k,
    v,
    top,
    total,
    acc,
    att,
    own_shift,
    other_shift,
    own_mask,
    other_mask,
):
    p = lax.axis_index("mp")
    first_kernel(normed, w, count_here, q, k, v, top, total, acc, att)
    mask_shift(own_base, p, count_here, own_shift, own_mask)
    mask_shift(other_base, 1 - p, count_here, other_shift, other_mask)


def halo_kernel(halo, frames, gain, bias, wo, *refs):
    parts = (refs[:8], refs[8:16])
    send, att_all, normed, kx, vx = refs[16:]
    p = lax.axis_index("mp")
    last = lax.axis_size("tm") - 1
    tm = lax.axis_index("tm")
    rows, queries, keys = frames.shape[0], refs[1].shape[0], refs[2].shape[0]
    width = refs[1].shape[1]
    heads = width // HEAD_DIM
    present = jnp.where(p == 0, tm > 0, tm < last)
    norms = (gain[...], bias[...])
    blocks = range(frames.shape[1] // LANES)
    ext = halo_rows(halo, (CTX - EXT) * (1 - p), EXT, blocks)
    row = positions(ext.shape, 0, 0)
    fixed = jnp.where(row == 0, gain[...], jnp.where(row == 1, bias[...], 0.0))
    left = jnp.concatenate([ext * gain[...], fixed], axis=0)
    high = left.astype(BF16)
    left = left - high.astype(F32)
    middle = left.astype(BF16)
    low = (left - middle.astype(F32)).astype(BF16)
    left = jnp.concatenate([high, middle, low], axis=0)
    ext_mean = jnp.mean(ext, axis=-1, keepdims=True)
    ext_center = ext - ext_mean
    ext_scale = lax.rsqrt(jnp.mean(ext_center * ext_center, axis=-1, keepdims=True) + 1e-05)
    q_ext = []
    for w, *_ in parts:
        thirds = dot(left, w[0])
        whole = thirds[: 2 * EXT] + thirds[2 * EXT : 4 * EXT] + thirds[4 * EXT :]
        q = (whole[:EXT] - ext_mean * whole[EXT : EXT + 1]) * ext_scale
        q_ext.append((q + whole[EXT + 1 : EXT + 2]) * SCALE)
    q_ext = jnp.concatenate(q_ext, axis=1)
    near = halo_rows(halo, 0, CTX, blocks)
    normed[:CTX, :] = layer_normed(near, *norms).astype(BF16)
    far = halo[len(blocks) * CTX :, :].astype(F32)
    far = jnp.concatenate([far[i * FAR : (i + 1) * FAR] for i in blocks], axis=1)
    far = jnp.concatenate([far, jnp.zeros((EXT - FAR, far.shape[1]), F32)], axis=0)
    normed[CTX:, :] = layer_normed(far, *norms).astype(BF16)
    near_at = jnp.where(p == 0, -CTX, rows)
    far_at = jnp.where(p == 0, -(CTX + FAR), rows + CTX)
    ext_at = jnp.where(p == 0, -EXT, rows)
    part = rows_at(p * (queries - CTX), CTX)
    rest = rows_at((1 - p) * CTX, queries - CTX)
    own = rows_at(p * (keys - CTX), CTX)
    own_pos = p * (rows - CTX)
    blank = jnp.zeros((PAD - EXT, width), F32)
    query_pos = positions((CTX, CTX), 0, p * (rows - CTX))
    near_pos = positions((CTX, CTX), 1, near_at)
    allowed = (jnp.abs(near_pos - query_pos) <= CTX) & present
    each = [
        (side, head, slice(head * HEAD_DIM, (head + 1) * HEAD_DIM))
        for side in range(2)
        for head in range(heads)
    ]

    def lanes_of(side, at):
        return slice(side * width + at.start, side * width + at.stop)

    for side, (w, q, k, v, top_own, total_own, acc_own, att) in enumerate(parts):
        to = slice(side * width, (side + 1) * width)
        kx[CTX + PAD :, to] = k[own, :]
        vx[CTX + PAD :, to] = v[own, :]
        att_all[CTX + PAD : CTX + PAD + queries - CTX, to] = att[rest, :]

    def project(x, i, sides):
        for side in sides:
            w = parts[side][0]
            to = slice(side * width, (side + 1) * width)
            got = dot(normed[...], w[i])
            x[:CTX, to] = got[:CTX].astype(BF16)
            x[CTX : CTX + PAD, to] = jnp.concatenate([got[CTX:], blank], axis=0).astype(BF16)

    scores = []
    project(kx, 1, (0, 1))
    deep = 2 * heads * EXT
    tiled = jnp.concatenate([q_ext] * (2 * heads), axis=0)
    head_of_row = positions(tiled.shape, 0, 0) // EXT
    head_of_lane = positions(tiled.shape, 1, 0) // HEAD_DIM
    tiled = jnp.where(head_of_row == head_of_lane, tiled, 0.0).astype(BF16)
    project(vx, 2, (0,))
    scores += [
        dot_t(parts[i][1][part, at], kx[:CTX, lanes_of(i, at)]) for i, head, at in each if i == 0
    ]
    scores += [
        dot_t(parts[i][1][part, at], kx[:CTX, lanes_of(i, at)]) for i, head, at in each if i == 1
    ]
    ext_scores = dot_t(tiled, kx[...])
    project(vx, 2, (1,))
    raised, total, faded = [], [], []
    for (side, head, at), score in zip(each, scores):
        top_own, total_own = parts[side][4], parts[side][5]
        score = jnp.where(allowed, score, NEG)
        before = top_own[head, part, :]
        top = jnp.maximum(before, jnp.max(score, axis=-1, keepdims=True))
        up = jnp.exp2(score - top)
        faded.append(jnp.exp2(before - top))
        total.append(
            total_own[head, part, :] * faded[-1] + jnp.sum(up, axis=-1, keepdims=True)
        )
        raised.append(up.astype(BF16))
    column = positions((deep, SPAN), 1, 0)
    key_pos = jnp.where(
        column < CTX,
        column + near_at,
        jnp.where(column < CTX + FAR, column - CTX + far_at, column - (CTX + PAD) + own_pos),
    )
    row_pos = positions((deep, SPAN), 0, 0) % EXT + ext_at
    seen = (jnp.abs(key_pos - row_pos) <= CTX) & ((column < CTX + FAR) | (column >= CTX + PAD))
    ext_scores = jnp.where(seen, ext_scores, NEG)
    ext_up = jnp.exp2(ext_scores - jnp.max(ext_scores, axis=-1, keepdims=True))
    ext_total = jnp.sum(ext_up, axis=-1, keepdims=True)
    gathered = [
        dot(up, vx[:CTX, lanes_of(side, at)]) for (side, head, at), up in zip(each, raised)
    ]
    spread = dot(ext_up.astype(BF16), vx[...]) * (1.0 / ext_total)
    for i, (side, head, at) in enumerate(each):
        acc = parts[side][6][part, at] * faded[i] + gathered[i]
        att_all[:CTX, lanes_of(side, at)] = (acc / total[i]).astype(BF16)
    ext_att = jnp.concatenate(
        [
            spread[h * EXT : (h + 1) * EXT, h * HEAD_DIM : (h + 1) * HEAD_DIM]
            for h in range(2 * heads)
        ],
        axis=1,
    )
    att_all[CTX : CTX + PAD, :] = jnp.concatenate(
        [ext_att, jnp.zeros_like(ext_att)], axis=0
    ).astype(BF16)
    mix(att_all, frames, halo, wo, 1 - p, send)


def mix(att_all, frames, halo, wo, columns, out):
    p = lax.axis_index("mp")
    rows, width = frames.shape[0], out.shape[1]
    queries = out.shape[0] - EXT
    other = queries - CTX
    lanes = pl.ds(pl.multiple_of(columns * width, width), width)
    projected = 0.0
    for side in range(2):
        for at in range(0, width, 2 * HEAD_DIM):
            first = (p if side == 0 else 1 - p) * width + at
            pair = wo[pl.ds(pl.multiple_of(first, 128), 2 * HEAD_DIM), :]
            at += side * width
            projected = projected + dot(att_all[:, at : at + 2 * HEAD_DIM], pair)

    def put(plain, to, size, at):
        out[rows_at(to, size), :] = (plain + projected[at : at + size]).astype(BF16)

    def own(at, size):
        return frames[rows_at(p * (rows - queries) + at, size), lanes].astype(F32)

    put(own(p * other, CTX), p * other, CTX, 0)
    count = width // LANES
    blocks = [columns * count + i for i in range(count)]
    put(halo_rows(halo, (CTX - EXT) * (1 - p), EXT, blocks), queries, EXT, CTX)
    put(own((1 - p) * CTX, other), (1 - p) * CTX, other, CTX + PAD)


def keep_kernel(att_all, frames, halo, wo, keep):
    mix(att_all, frames, halo, wo, lax.axis_index("mp"), keep)


def convolved(block, core, shift_by, mask, weight, scale, shift, store):
    half = shift_by.shape[0] // len(MOVED)
    rows = rows_at(core * (block.shape[0] - EXT - half), half)
    step = 2 * LANES
    valid = jnp.concatenate([mask[rows, :]] * (step // mask.shape[1]), axis=1)
    for at in range(0, block.shape[1], step):
        lanes = slice(at, at + step)
        gain = 0.5 * scale[:, lanes]
        plain = block[rows, lanes].astype(F32)
        u = plain * valid * (weight[MIDDLE : MIDDLE + 1, lanes] * gain) + 0.5 * shift[:, lanes]
        for first in range(0, len(MOVED), GROUP):
            group = MOVED[first : first + GROUP]
            moved = dot(shift_by[first * half : (first + len(group)) * half, :], block[:, lanes])
            for i, tap in enumerate(group):
                part = moved[i * half : (i + 1) * half]
                u = u + part * (weight[tap : tap + 1, lanes] * gain)
        store(lanes, (plain + (u + u * jnp.tanh(u))).astype(BF16))


def own_conv_kernel(keep, shift_by, mask, weight, scale, shift, out):
    def store(lanes, value):
        out[:, lanes] = value

    core = lax.axis_index("mp")
    convolved(keep, core, shift_by, mask, weight, scale, shift, store)


def other_conv_kernel(got, done, shift_by, mask, weight, scale, shift, out, block, sems):
    core = 1 - lax.axis_index("mp")
    half = done.shape[0]
    first = pltpu.make_async_copy(done, out.at[rows_at((1 - core) * half, half), :], sems.at[0])
    first.start()
    copies = [first]

    def store(lanes, value):
        block[:, lanes] = value
        copies.append(
            pltpu.make_async_copy(
                block.at[:, lanes], out.at[rows_at(core * half, half), lanes], sems.at[len(copies)]
            )
        )
        copies[-1].start()

    convolved(got, core, shift_by, mask, weight, scale, shift, store)
    for copy in copies:
        copy.wait()


def call(kernel, out_shape, in_specs, out_specs, scratch=(), flops=0, size=0, exps=0, limit=16):
    return pl.pallas_call(
        kernel,
        out_shape=out_shape,
        in_specs=in_specs,
        out_specs=out_specs,
        scratch_shapes=scratch,
        compiler_params=pltpu.CompilerParams(vmem_limit_bytes=limit << 20),
        cost_estimate=pl.CostEstimate(flops=flops, bytes_accessed=size, transcendentals=exps),
    )


def compute(frames, valid, norm_gain, norm_bias, w_qkv, w_out, conv_weight, conv_scale, conv_shift):
    rows, model = frames.shape
    width = w_qkv.shape[2]
    heads = width // HEAD_DIM
    count = lax.axis_size("tm")
    half = rows // 2
    queries = half + EXT
    keys = half + EXT + CTX
    block = queries + EXT
    assert rows >= HALO + CTX and rows % 32 == 0
    shaped = jax.ShapeDtypeStruct
    pairs = [(1, 0), (2 * count - 2, 2 * count - 1)]
    for i in range(count - 1):
        pairs += [(2 * i, 2 * (i + 1)), (2 * (i + 1) + 1, 2 * i + 1)]
    other = [(0, 1), (1, 0)]
    shift_shapes = (shaped((len(MOVED) * half, block), BF16),) * 2
    shifts = call(warm_kernel, shift_shapes, [], (VMEM,) * 2, flops=WARM_FLOPS)()
    sent = call(
        pick_kernel,
        shaped(((CTX + FAR) * (model // LANES), LANES), BF16),
        [VMEM, ANY],
        VMEM,
        flops=PICK_FLOPS,
    )(frames, shifts[0])
    halo = lax.ppermute(sent, ("tm", "mp"), pairs)
    w_other = lax.ppermute(w_qkv, "mp", other)
    wo_other = lax.ppermute(w_out, "mp", other)
    gain, bias = norm_gain.reshape(1, model), norm_bias.reshape(1, model)
    results = (
        shaped((queries, width), BF16),
        shaped((keys, width), BF16),
        shaped((keys, width), BF16),
        shaped((heads, queries, HEAD_DIM), F32),
        shaped((heads, queries, HEAD_DIM), F32),
        shaped((queries, width), F32),
        shaped((queries, width), BF16),
    )
    normed, count_here = call(
        norm_kernel,
        (shaped((keys, model), BF16), shaped((8, 256), jnp.int32)),
        [VMEM, SMEM, VMEM, VMEM],
        (VMEM,) * 2,
        flops=NORM_FLOPS,
        size=1_000_000,
    )(frames, valid, gain, bias)
    mine = call(
        first_kernel,
        results,
        [VMEM] * 3,
        (VMEM,) * 7,
        flops=1_300_000_000,
        size=4_000_000,
        exps=300_000,
    )(normed, w_qkv, count_here)
    second = call(
        second_kernel,
        results + shift_shapes + (shaped((block, LANES), F32),) * 2,
        [VMEM] * 5,
        (VMEM,) * 11,
        flops=1_300_000_000,
        size=4_000_000,
        exps=300_000,
    )(normed, w_other, count_here, *shifts)
    theirs, (own_shift, other_shift, own_mask, other_mask) = second[:7], second[7:]
    send, att_all = call(
        halo_kernel,
        (shaped((block, width), BF16), shaped((pl.cdiv(queries, 16) * 16 + PAD, model), BF16)),
        [VMEM] * 21,
        (VMEM,) * 2,
        [
            pltpu.VMEM((HALO, model), BF16),
            pltpu.VMEM((SPAN, model), BF16),
            pltpu.VMEM((SPAN, model), BF16),
        ],
        flops=1_500_000_000,
        size=10_000_000,
        exps=300_000,
    )(halo, frames, gain, bias, wo_other, w_qkv, *mine, w_other, *theirs)
    got = lax.ppermute(send, "mp", other)
    keep = call(
        keep_kernel,
        shaped((block, width), BF16),
        [VMEM] * 4,
        VMEM,
        flops=200_000_000,
        size=1_000_000,
    )(att_all, frames, halo, w_out)
    weights = (conv_weight, conv_scale.reshape(1, width), conv_shift.reshape(1, width))
    done = call(
        own_conv_kernel,
        shaped((half, width), BF16),
        [VMEM] * 6,
        VMEM,
        flops=270_000_000,
        size=1_000_000,
    )(keep, own_shift, own_mask, *weights)
    return call(
        other_conv_kernel,
        shaped((rows, width), BF16),
        [VMEM] * 7,
        ANY,
        [pltpu.VMEM((half, width), BF16), pltpu.SemaphoreType.DMA((1 + width // 256,))],
        flops=270_000_000,
        size=1_000_000,
    )(got, done, other_shift, other_mask, *weights)


def solution(mesh):
    placed = (
        P("tm", None),
        P("tm"),
        P(),
        P(),
        P(None, None, "mp"),
        P(None, "mp"),
        P(None, "mp"),
        P("mp"),
        P("mp"),
    )
    return jax.shard_map(
        compute, mesh=mesh, in_specs=placed, out_specs=P("tm", "mp"), check_vma=False
    )
```

```python
import math

import jax
import jax.numpy as jnp
from jax import lax
from jax.experimental import pallas as pl
from jax.experimental.pallas import tpu as pltpu
from jax.sharding import PartitionSpec as P

HEAD_DIM = 128
CTX = 128
KERNEL = 9
EXT = 8
HALO = CTX + EXT
FAR = KERNEL // 2
LANES = 128
MIDDLE = KERNEL // 2
MOVED = [tap for tap in range(KERNEL) if tap != MIDDLE]
PAD = 16
SPAN = CTX + PAD + CTX
NEG = -1e30
GROUP = 2
WARM_FLOPS, PICK_FLOPS, NORM_FLOPS = 1_500_000_000, 1_000_000_000, 1_500_000_000
SCALE = math.log2(math.e) / math.sqrt(HEAD_DIM)
VMEM = pl.BlockSpec(memory_space=pltpu.VMEM)
ANY = pl.BlockSpec(memory_space=pl.ANY)
SMEM = pl.BlockSpec(memory_space=pltpu.SMEM)
F32, BF16 = jnp.float32, jnp.bfloat16


def layer_normed(values, gain, bias):
    center = values - jnp.mean(values, axis=-1, keepdims=True)
    spread = jnp.mean(center * center, axis=-1, keepdims=True)
    return center * lax.rsqrt(spread + 1e-05) * gain + bias


def norm_rows(source, source_at, target, target_at, count, gain, bias):
    step = 16
    for at in range(0, count, step):
        size = min(step, count - at)
        values = source[rows_at(source_at + at, size), :].astype(F32)
        target[target_at + at : target_at + at + size, :] = layer_normed(
            values, gain, bias
        ).astype(BF16)


def dot(a, b):
    return jnp.dot(a, b, preferred_element_type=F32)


def dot_t(a, b):
    return lax.dot_general(a, b, (((1,), (1,)), ((), ())), preferred_element_type=F32)


def positions(shape, dim, start):
    return lax.broadcasted_iota(jnp.int32, shape, dim) + start


def rows_at(start, size):
    return pl.ds(pl.multiple_of(start, 8), size)


def lane_blocks(width):
    return [slice(at, at + LANES) for at in range(0, width, LANES)]


def pick_kernel(frames, after, sent):
    p = lax.axis_index("mp")
    rows, width = frames.shape
    blocks = lane_blocks(width)
    near = rows_at((1 - p) * (rows - CTX), CTX)
    for i, lanes in enumerate(blocks):
        sent[i * CTX : (i + 1) * CTX, :] = frames[near, lanes]
    far = frames[rows_at((1 - p) * (rows - HALO) + p * CTX, EXT), :].astype(F32)
    far = jnp.where(p == 0, pltpu.roll(far, EXT - FAR, 0), far)
    sent[len(blocks) * CTX :, :] = jnp.concatenate(
        [far[:FAR, lanes] for lanes in blocks], axis=0
    ).astype(BF16)


def halo_rows(halo, start, size, blocks):
    return jnp.concatenate(
        [halo[rows_at(i * CTX + start, size), :].astype(F32) for i in blocks], axis=1
    )


def own_heads(
    normed, w, count, q_out, k_out, v_out, top_out, total_out, acc_out, att_out, edge_out
):
    p = lax.axis_index("mp")
    keys, queries = k_out.shape[0], q_out.shape[0]
    rows = 2 * (queries - EXT)
    key_at, query_at = p * (rows - keys), p * (rows - queries)
    k_out[...] = dot(normed[...], w[1]).astype(BF16)
    picked = normed[pl.ds(pl.multiple_of(p * (keys - queries), 16), queries), :]
    q_out[...] = (dot(picked, w[0]) * SCALE).astype(BF16)
    v_out[...] = dot(normed[...], w[2]).astype(BF16)
    edge = k_out[rows_at(p * (keys - CTX), CTX), :].astype(F32)
    edge_out[...] = edge.T.astype(BF16)
    key_pos = positions((queries, keys), 1, key_at)
    query_pos = positions((queries, keys), 0, query_at)
    allowed = (jnp.abs(key_pos - query_pos) <= CTX) & (key_pos < count)
    heads = [slice(at, at + HEAD_DIM) for at in range(0, q_out.shape[1], HEAD_DIM)]
    scores = [dot_t(q_out[:, at], k_out[:, at]) for at in heads]
    raised, totals = [], []
    for head, score in enumerate(scores):
        score = jnp.where(allowed, score, NEG)
        top = jnp.max(score, axis=-1, keepdims=True)
        up = jnp.exp2(score - top)
        total = jnp.sum(up, axis=-1, keepdims=True)
        top_out[head] = jnp.broadcast_to(top, (queries, HEAD_DIM))
        total_out[head] = jnp.broadcast_to(total, (queries, HEAD_DIM))
        raised.append(up.astype(BF16))
        totals.append(total)
    for head, at in enumerate(heads):
        acc = dot(raised[head], v_out[:, at])
        acc_out[:, at] = acc
        att_out[:, at] = (acc * (1.0 / totals[head])).astype(BF16)


def norm_kernel(frames, valid, gain, bias, normed, count_here):
    p = lax.axis_index("mp")
    rows, keys = frames.shape[0], normed.shape[0]
    low, high = jnp.int32(0), jnp.int32(rows)
    for _ in range(rows.bit_length()):
        middle = (low + high) // 2
        one = valid[jnp.minimum(middle, rows - 1)] > 0
        open_ = low < high
        low = jnp.where(open_ & one, middle + 1, low)
        high = jnp.where(open_ & jnp.logical_not(one), middle, high)
    count_here[...] = jnp.full(count_here.shape, low, jnp.int32)
    norm_rows(frames, p * (rows - keys), normed, 0, keys, gain[...], bias[...])


def first_kernel(normed, w, count_here, q, k, v, top, total, acc, att, edge):
    keys = k.shape[0]
    count = jnp.concatenate([count_here[0:1, :]] * pl.cdiv(keys, count_here.shape[1]), axis=1)[:, :keys]
    own_heads(normed, w, count, q, k, v, top, total, acc, att, edge)


def block_time(index, core, queries, rows):
    edge = jnp.where(core == 0, -EXT, rows)
    return jnp.where(index < queries, index + core * (rows - queries), index - queries + edge)


def block_mask(index, core, queries, rows, count):
    tm, last = lax.axis_index("tm"), lax.axis_size("tm") - 1
    time = block_time(index, core, queries, rows)
    low = jnp.where(tm > 0, -EXT, 0)
    high = jnp.where(tm < last, rows + EXT, count)
    return jnp.where((time >= low) & (time < high), 1.0, 0.0)


def warm_kernel(own_shift, other_shift):
    p = lax.axis_index("mp")
    for out, core in ((own_shift, p), (other_shift, 1 - p)):
        half, width = out.shape[0] // len(MOVED), out.shape[1]
        time = block_time(positions((1, width), 1, 0), core, width - EXT, 2 * half)
        for i, tap in enumerate(MOVED):
            row = positions((half, width), 0, core * half + tap - KERNEL // 2)
            out[i * half : (i + 1) * half, :] = jnp.where(row == time, 1.0, 0.0).astype(BF16)


def mask_shift(shift, core, count, out, mask_out):
    half, width = out.shape[0] // len(MOVED), out.shape[1]
    queries, rows = width - EXT, 2 * half
    mask = block_mask(positions((1, width), 1, 0), core, queries, rows, count[0:1, :width])
    mask = mask.astype(BF16)
    for i in range(len(MOVED)):
        at = slice(i * half, (i + 1) * half)
        out[at, :] = shift[at, :] * mask
    index = positions(mask_out.shape, 0, 0)
    mask_out[...] = block_mask(index, core, queries, rows, count[0:1, : mask_out.shape[1]])


def second_kernel(
    normed,
    w,
    count_here,
    own_base,
    other_base,
    q,
    k,
    v,
    top,
    total,
    acc,
    att,
    edge,
    own_shift,
    other_shift,
    own_mask,
    other_mask,
):
    p = lax.axis_index("mp")
    first_kernel(normed, w, count_here, q, k, v, top, total, acc, att, edge)
    mask_shift(own_base, p, count_here, own_shift, own_mask)
    mask_shift(other_base, 1 - p, count_here, other_shift, other_mask)


def halo_kernel(halo, frames, gain, bias, wo, *refs):
    parts = (refs[:9], refs[9:18])
    send, att_all, normed, kx, vx = refs[18:]
    p = lax.axis_index("mp")
    last = lax.axis_size("tm") - 1
    tm = lax.axis_index("tm")
    rows, queries, keys = frames.shape[0], refs[1].shape[0], refs[2].shape[0]
    width = refs[1].shape[1]
    heads = width // HEAD_DIM
    present = jnp.where(p == 0, tm > 0, tm < last)
    norms = (gain[...], bias[...])
    blocks = range(frames.shape[1] // LANES)
    ext = halo_rows(halo, (CTX - EXT) * (1 - p), EXT, blocks)
    row = positions(ext.shape, 0, 0)
    fixed = jnp.where(row == 0, gain[...], jnp.where(row == 1, bias[...], 0.0))
    left = jnp.concatenate([ext * gain[...], fixed], axis=0)
    high = left.astype(BF16)
    left = left - high.astype(F32)
    middle = left.astype(BF16)
    low = (left - middle.astype(F32)).astype(BF16)
    left = jnp.concatenate([high, middle, low], axis=0)
    ext_mean = jnp.mean(ext, axis=-1, keepdims=True)
    ext_center = ext - ext_mean
    ext_scale = lax.rsqrt(jnp.mean(ext_center * ext_center, axis=-1, keepdims=True) + 1e-05)
    q_ext = []
    for w, *_ in parts:
        thirds = dot(left, w[0])
        whole = thirds[: 2 * EXT] + thirds[2 * EXT : 4 * EXT] + thirds[4 * EXT :]
        q = (whole[:EXT] - ext_mean * whole[EXT : EXT + 1]) * ext_scale
        q_ext.append((q + whole[EXT + 1 : EXT + 2]) * SCALE)
    q_ext = jnp.concatenate(q_ext, axis=1)
    near = halo_rows(halo, 0, CTX, blocks)
    normed[:CTX, :] = layer_normed(near, *norms).astype(BF16)
    far = halo[len(blocks) * CTX :, :].astype(F32)
    far = jnp.concatenate([far[i * FAR : (i + 1) * FAR] for i in blocks], axis=1)
    far = jnp.concatenate([far, jnp.zeros((EXT - FAR, far.shape[1]), F32)], axis=0)
    normed[CTX:, :] = layer_normed(far, *norms).astype(BF16)
    near_at = jnp.where(p == 0, -CTX, rows)
    far_at = jnp.where(p == 0, -(CTX + FAR), rows + CTX)
    ext_at = jnp.where(p == 0, -EXT, rows)
    part = rows_at(p * (queries - CTX), CTX)
    rest = rows_at((1 - p) * CTX, queries - CTX)
    own = rows_at(p * (keys - CTX), CTX)
    own_pos = p * (rows - CTX)
    blank = jnp.zeros((PAD - EXT, width), F32)
    query_pos = positions((CTX, CTX), 0, p * (rows - CTX))
    near_pos = positions((CTX, CTX), 1, near_at)
    allowed = (jnp.abs(near_pos - query_pos) <= CTX) & present
    each = [
        (side, head, slice(head * HEAD_DIM, (head + 1) * HEAD_DIM))
        for side in range(2)
        for head in range(heads)
    ]

    def lanes_of(side, at):
        return slice(side * width + at.start, side * width + at.stop)

    for side, (w, q, k, v, top_own, total_own, acc_own, att, edge) in enumerate(parts):
        to = slice(side * width, (side + 1) * width)
        vx[:CTX, to] = v[own, :]
        att_all[CTX + PAD : CTX + PAD + queries - CTX, to] = att[rest, :]

    def project(x, i, sides):
        for side in sides:
            w = parts[side][0]
            to = slice(side * width, (side + 1) * width)
            got = dot(normed[...], w[i])
            base = x.shape[0] - CTX - PAD
            x[base : base + CTX, to] = got[:CTX].astype(BF16)
            x[base + CTX :, to] = jnp.concatenate([got[CTX:], blank], axis=0).astype(BF16)

    scores = []
    project(kx, 1, (0, 1))
    deep = 2 * heads * EXT
    tiled = jnp.concatenate([q_ext] * (2 * heads), axis=0)
    head_of_row = positions(tiled.shape, 0, 0) // EXT
    head_of_lane = positions(tiled.shape, 1, 0) // HEAD_DIM
    tiled = jnp.where(head_of_row == head_of_lane, tiled, 0.0).astype(BF16)
    project(vx, 2, (0,))
    scores += [
        dot_t(parts[i][1][part, at], kx[:CTX, lanes_of(i, at)]) for i, head, at in each if i == 0
    ]
    scores += [
        dot_t(parts[i][1][part, at], kx[:CTX, lanes_of(i, at)]) for i, head, at in each if i == 1
    ]
    edges = jnp.concatenate([part[8][...] for part in parts], axis=0)
    ext_scores = jnp.concatenate([dot(tiled, edges), dot_t(tiled, kx[...])], axis=1)
    project(vx, 2, (1,))
    raised, total, faded = [], [], []
    for (side, head, at), score in zip(each, scores):
        top_own, total_own = parts[side][4], parts[side][5]
        score = jnp.where(allowed, score, NEG)
        before = top_own[head, part, :]
        top = jnp.maximum(before, jnp.max(score, axis=-1, keepdims=True))
        up = jnp.exp2(score - top)
        faded.append(jnp.exp2(before - top))
        total.append(
            total_own[head, part, :] * faded[-1] + jnp.sum(up, axis=-1, keepdims=True)
        )
        raised.append(up.astype(BF16))
    column = positions((deep, SPAN), 1, 0)
    key_pos = jnp.where(
        column < CTX,
        column + own_pos,
        jnp.where(column < 2 * CTX, column - CTX + near_at, column - 2 * CTX + far_at),
    )
    row_pos = positions((deep, SPAN), 0, 0) % EXT + ext_at
    seen = (jnp.abs(key_pos - row_pos) <= CTX) & (column < 2 * CTX + FAR)
    ext_scores = jnp.where(seen, ext_scores, NEG)
    ext_up = jnp.exp2(ext_scores - jnp.max(ext_scores, axis=-1, keepdims=True))
    ext_total = jnp.sum(ext_up, axis=-1, keepdims=True)
    gathered = [
        dot(up, vx[CTX : 2 * CTX, lanes_of(side, at)]) for (side, head, at), up in zip(each, raised)
    ]
    spread = dot(ext_up.astype(BF16), vx[...]) * (1.0 / ext_total)
    for i, (side, head, at) in enumerate(each):
        acc = parts[side][6][part, at] * faded[i] + gathered[i]
        att_all[:CTX, lanes_of(side, at)] = (acc / total[i]).astype(BF16)
    ext_att = jnp.concatenate(
        [
            spread[h * EXT : (h + 1) * EXT, h * HEAD_DIM : (h + 1) * HEAD_DIM]
            for h in range(2 * heads)
        ],
        axis=1,
    )
    att_all[CTX : CTX + PAD, :] = jnp.concatenate(
        [ext_att, jnp.zeros_like(ext_att)], axis=0
    ).astype(BF16)
    mix(att_all, frames, halo, wo, 1 - p, send)


def mix(att_all, frames, halo, wo, columns, out):
    p = lax.axis_index("mp")
    rows, width = frames.shape[0], out.shape[1]
    queries = out.shape[0] - EXT
    other = queries - CTX
    lanes = pl.ds(pl.multiple_of(columns * width, width), width)
    projected = 0.0
    for side in range(2):
        for at in range(0, width, 2 * HEAD_DIM):
            first = (p if side == 0 else 1 - p) * width + at
            pair = wo[pl.ds(pl.multiple_of(first, 128), 2 * HEAD_DIM), :]
            at += side * width
            projected = projected + dot(att_all[:, at : at + 2 * HEAD_DIM], pair)

    def put(plain, to, size, at):
        out[rows_at(to, size), :] = (plain + projected[at : at + size]).astype(BF16)

    def own(at, size):
        return frames[rows_at(p * (rows - queries) + at, size), lanes].astype(F32)

    put(own(p * other, CTX), p * other, CTX, 0)
    count = width // LANES
    blocks = [columns * count + i for i in range(count)]
    put(halo_rows(halo, (CTX - EXT) * (1 - p), EXT, blocks), queries, EXT, CTX)
    put(own((1 - p) * CTX, other), (1 - p) * CTX, other, CTX + PAD)


def keep_kernel(att_all, frames, halo, wo, keep):
    mix(att_all, frames, halo, wo, lax.axis_index("mp"), keep)


def convolved(block, core, shift_by, mask, weight, scale, shift, store):
    half = shift_by.shape[0] // len(MOVED)
    rows = rows_at(core * (block.shape[0] - EXT - half), half)
    step = 2 * LANES
    valid = jnp.concatenate([mask[rows, :]] * (step // mask.shape[1]), axis=1)
    for at in range(0, block.shape[1], step):
        lanes = slice(at, at + step)
        gain = 0.5 * scale[:, lanes]
        plain = block[rows, lanes].astype(F32)
        u = plain * valid * (weight[MIDDLE : MIDDLE + 1, lanes] * gain) + 0.5 * shift[:, lanes]
        for first in range(0, len(MOVED), GROUP):
            group = MOVED[first : first + GROUP]
            moved = dot(shift_by[first * half : (first + len(group)) * half, :], block[:, lanes])
            for i, tap in enumerate(group):
                part = moved[i * half : (i + 1) * half]
                u = u + part * (weight[tap : tap + 1, lanes] * gain)
        store(lanes, (plain + (u + u * jnp.tanh(u))).astype(BF16))


def own_conv_kernel(keep, shift_by, mask, weight, scale, shift, out):
    def store(lanes, value):
        out[:, lanes] = value

    core = lax.axis_index("mp")
    convolved(keep, core, shift_by, mask, weight, scale, shift, store)


def other_conv_kernel(got, done, shift_by, mask, weight, scale, shift, out, block, sems):
    core = 1 - lax.axis_index("mp")
    half = done.shape[0]
    first = pltpu.make_async_copy(done, out.at[rows_at((1 - core) * half, half), :], sems.at[0])
    first.start()
    copies = [first]

    def store(lanes, value):
        block[:, lanes] = value
        copies.append(
            pltpu.make_async_copy(
                block.at[:, lanes], out.at[rows_at(core * half, half), lanes], sems.at[len(copies)]
            )
        )
        copies[-1].start()

    convolved(got, core, shift_by, mask, weight, scale, shift, store)
    for copy in copies:
        copy.wait()


def call(kernel, out_shape, in_specs, out_specs, scratch=(), flops=0, size=0, exps=0, limit=16):
    return pl.pallas_call(
        kernel,
        out_shape=out_shape,
        in_specs=in_specs,
        out_specs=out_specs,
        scratch_shapes=scratch,
        compiler_params=pltpu.CompilerParams(vmem_limit_bytes=limit << 20),
        cost_estimate=pl.CostEstimate(flops=flops, bytes_accessed=size, transcendentals=exps),
    )


def compute(frames, valid, norm_gain, norm_bias, w_qkv, w_out, conv_weight, conv_scale, conv_shift):
    rows, model = frames.shape
    width = w_qkv.shape[2]
    heads = width // HEAD_DIM
    count = lax.axis_size("tm")
    half = rows // 2
    queries = half + EXT
    keys = half + EXT + CTX
    block = queries + EXT
    assert rows >= HALO + CTX and rows % 32 == 0
    shaped = jax.ShapeDtypeStruct
    pairs = [(1, 0), (2 * count - 2, 2 * count - 1)]
    for i in range(count - 1):
        pairs += [(2 * i, 2 * (i + 1)), (2 * (i + 1) + 1, 2 * i + 1)]
    other = [(0, 1), (1, 0)]
    shift_shapes = (shaped((len(MOVED) * half, block), BF16),) * 2
    shifts = call(warm_kernel, shift_shapes, [], (VMEM,) * 2, flops=WARM_FLOPS)()
    sent = call(
        pick_kernel,
        shaped(((CTX + FAR) * (model // LANES), LANES), BF16),
        [VMEM, ANY],
        VMEM,
        flops=PICK_FLOPS,
    )(frames, shifts[0])
    halo = lax.ppermute(sent, ("tm", "mp"), pairs)
    w_other = lax.ppermute(w_qkv, "mp", other)
    wo_other = lax.ppermute(w_out, "mp", other)
    gain, bias = norm_gain.reshape(1, model), norm_bias.reshape(1, model)
    results = (
        shaped((queries, width), BF16),
        shaped((keys, width), BF16),
        shaped((keys, width), BF16),
        shaped((heads, queries, HEAD_DIM), F32),
        shaped((heads, queries, HEAD_DIM), F32),
        shaped((queries, width), F32),
        shaped((queries, width), BF16),
        shaped((width, CTX), BF16),
    )
    normed, count_here = call(
        norm_kernel,
        (shaped((keys, model), BF16), shaped((8, 256), jnp.int32)),
        [VMEM, SMEM, VMEM, VMEM],
        (VMEM,) * 2,
        flops=NORM_FLOPS,
        size=1_000_000,
    )(frames, valid, gain, bias)
    mine = call(
        first_kernel,
        results,
        [VMEM] * 3,
        (VMEM,) * 8,
        flops=1_300_000_000,
        size=4_000_000,
        exps=300_000,
    )(normed, w_qkv, count_here)
    second = call(
        second_kernel,
        results + shift_shapes + (shaped((block, LANES), F32),) * 2,
        [VMEM] * 5,
        (VMEM,) * 12,
        flops=1_300_000_000,
        size=4_000_000,
        exps=300_000,
    )(normed, w_other, count_here, *shifts)
    theirs, (own_shift, other_shift, own_mask, other_mask) = second[:8], second[8:]
    send, att_all = call(
        halo_kernel,
        (shaped((block, width), BF16), shaped((pl.cdiv(queries, 16) * 16 + PAD, model), BF16)),
        [VMEM] * 23,
        (VMEM,) * 2,
        [
            pltpu.VMEM((HALO, model), BF16),
            pltpu.VMEM((CTX + PAD, model), BF16),
            pltpu.VMEM((SPAN, model), BF16),
        ],
        flops=1_500_000_000,
        size=10_000_000,
        exps=300_000,
    )(halo, frames, gain, bias, wo_other, w_qkv, *mine, w_other, *theirs)
    got = lax.ppermute(send, "mp", other)
    keep = call(
        keep_kernel,
        shaped((block, width), BF16),
        [VMEM] * 4,
        VMEM,
        flops=200_000_000,
        size=1_000_000,
    )(att_all, frames, halo, w_out)
    weights = (conv_weight, conv_scale.reshape(1, width), conv_shift.reshape(1, width))
    done = call(
        own_conv_kernel,
        shaped((half, width), BF16),
        [VMEM] * 6,
        VMEM,
        flops=270_000_000,
        size=1_000_000,
    )(keep, own_shift, own_mask, *weights)
    return call(
        other_conv_kernel,
        shaped((rows, width), BF16),
        [VMEM] * 7,
        ANY,
        [pltpu.VMEM((half, width), BF16), pltpu.SemaphoreType.DMA((1 + width // 256,))],
        flops=270_000_000,
        size=1_000_000,
    )(got, done, other_shift, other_mask, *weights)


def solution(mesh):
    placed = (
        P("tm", None),
        P("tm"),
        P(),
        P(),
        P(None, None, "mp"),
        P(None, "mp"),
        P(None, "mp"),
        P("mp"),
        P("mp"),
    )
    return jax.shard_map(
        compute, mesh=mesh, in_specs=placed, out_specs=P("tm", "mp"), check_vma=False
    )
```
